32 devices in a mesh: dp: 8 (over y, x, core), chan: 4 (over z).
Axes of the slice: x: 2, y: 2, z: 4, core: 2. Of those that a mesh axis runs over, the one named last changes fastest.
Arguments:
- patches: bfloat16 [64, 256, 1280], P('dp', None, 'chan'), may hold values from -13 to 13
- cotangent: bfloat16 [64, 256, 1280], P('dp', None, 'chan'), may hold values from -33 to 33
- w_token_in: bfloat16 [640, 256], replicated, may hold values from -0.375 to 0.375
- b_token_in: float32 [640], replicated, may hold values from -3 to 3
- w_token_out: bfloat16 [256, 640], replicated, may hold values from -0.25 to 0.25
- layer_norm_gain: float32 [1280], replicated, may hold values from 0.25 to 1.75
- layer_norm_bias: float32 [1280], replicated, may hold values from -3 to 3
Outputs:
- grad_patches: bfloat16 [64, 256, 1280], P('dp', None, 'chan')
- grad_w_in: float32 [640, 256], replicated
- grad_w_out: float32 [256, 640], replicated
- grad_b_in: float32 [640], replicated
- grad_gain: float32 [1280], P('chan')
- grad_shift: float32 [1280], P('chan')
The draws below stay inside these ranges and needn't reach their ends.
All inputs are finite; a program needn't handle non-finite values.
Results may differ from the reference program's by a relative error of at most 0.0065.
Values may be sent and summed in bfloat16 or wider, within the bound.
No kernel may reach another device: no remote copies, remote signals or barrier semaphores. Data moves between devices by JAX's collectives and lax.ppermute only.
A program may use at most 64 MiB of HBM per device.

```python
import math
import jax
import jax.numpy as jnp
from jax import lax

CHANNEL_COUNT = 1280
P_SIZE = 256
HID = 640
IMG_DEV = 8
IMAGES = 64
N_DP = 8


def draw_patches(key, part):
    first_term, second_term = jax.random.split(key, 2)
    base = jnp.clip(jax.random.normal(first_term, (IMAGES, P_SIZE, CHANNEL_COUNT), jnp.float32), -4.0, 4.0)
    scale = jnp.exp(jax.random.uniform(second_term, (CHANNEL_COUNT,), jnp.float32, math.log(0.25), math.log(2.5)))
    values = base * scale
    return values.astype(jnp.bfloat16)


def draw_cotangent(key, part):
    first_term, second_term, third = jax.random.split(key, 3)
    base = jnp.clip(jax.random.normal(first_term, (IMAGES, P_SIZE, CHANNEL_COUNT), jnp.float32), -3.5, 3.5)
    shared = 1.5 * jnp.clip(jax.random.normal(third, (IMAGES, P_SIZE, 1), jnp.float32), -2.5, 2.5)
    rising = 3.0 ** (jnp.arange(IMAGES, dtype=jnp.float32) / max(IMAGES - 1, 1))
    channel = jnp.exp(jax.random.uniform(second_term, (CHANNEL_COUNT,), jnp.float32, -math.log(2.0), math.log(2.0)))
    values = (base * channel + shared) * rising[:, None, None]
    return values.astype(jnp.bfloat16)


def scatter_about(stream_key, dims, deviation, reach, held_as=jnp.bfloat16):
    return jnp.clip(deviation * jax.random.normal(stream_key, dims, jnp.float32), -reach, reach).astype(held_as)


def setup_inputs(seed: int = 0) -> dict:
    streams_of = jax.random.split(jax.random.key(seed), 8)
    return {
        "patches": draw_patches(jax.random.fold_in(streams_of[7], 71), 0),
        "cotangent": draw_cotangent(jax.random.fold_in(streams_of[7], 71), 0),
        "w_token_in": scatter_about(streams_of[2], (HID, P_SIZE), P_SIZE ** -0.5, 0.375),
        "b_token_in": scatter_about(streams_of[3], (HID,), 0.5, 3.0, jnp.float32),
        "w_token_out": scatter_about(streams_of[4], (P_SIZE, HID), HID ** -0.5, 0.25),
        "layer_norm_gain": jnp.clip(1.0 + 0.15 * jax.random.normal(streams_of[5], (CHANNEL_COUNT,), jnp.float32), 0.25, 1.75),
        "layer_norm_bias": scatter_about(streams_of[6], (CHANNEL_COUNT,), 0.5, 3.0, jnp.float32),
    }


eps_norm = 1e-05

def block_grads(xb, gb, w_token_in, b_token_in, w_token_out, layer_norm_gain, layer_norm_bias):
    hi = lax.Precision.HIGHEST
    input_float = xb.astype(jnp.float32)
    row_average = lax.optimization_barrier(jnp.sum(input_float, -1)) / CHANNEL_COUNT
    meansq = lax.optimization_barrier(jnp.sum(input_float * input_float, -1)) / CHANNEL_COUNT
    inverse_deviation = lax.rsqrt(meansq - row_average * row_average + eps_norm)
    centered_input = (input_float - row_average[..., None]) * inverse_deviation[..., None]
    normalized_output = (centered_input * layer_norm_gain + layer_norm_bias).astype(jnp.bfloat16)
    normed_f = normalized_output.astype(jnp.float32)
    w_in = w_token_in.astype(jnp.float32)
    w_out = w_token_out.astype(jnp.float32)
    pre = jnp.einsum('kp,bpc->bkc', w_in, normed_f, precision=hi) + b_token_in[None, :, None]
    cdf = 0.5 * (1.0 + jax.scipy.special.erf(pre / math.sqrt(2.0)))
    act = (pre * cdf).astype(jnp.bfloat16).astype(jnp.float32)
    slope = cdf + pre * jnp.exp(-0.5 * pre * pre) / math.sqrt(2.0 * math.pi)
    gradient_float = gb.astype(jnp.float32)
    grad_act = jnp.einsum('pk,bpc->bkc', w_out, gradient_float, precision=hi)
    grad_pre = (grad_act * slope).astype(jnp.bfloat16).astype(jnp.float32)
    gradient_normalized = jnp.einsum('kp,bkc->bpc', w_in, grad_pre, precision=hi).astype(jnp.bfloat16).astype(jnp.float32)
    dw_out = jnp.einsum('bpc,bkc->pk', gradient_float, act, precision=hi)
    dw_in = jnp.einsum('bkc,bpc->kp', grad_pre, normed_f, precision=hi)
    db_in = lax.optimization_barrier(jnp.sum(grad_pre, axis=(0, 2)))
    gain_gradient = lax.optimization_barrier(jnp.sum(gradient_normalized * centered_input, axis=(0, 1)))
    dshift = lax.optimization_barrier(jnp.sum(gradient_normalized, axis=(0, 1)))
    gradient_centered = gradient_normalized * layer_norm_gain
    first_term = lax.optimization_barrier(jnp.sum(gradient_centered, -1)) / CHANNEL_COUNT
    second_term = lax.optimization_barrier(jnp.sum(gradient_centered * centered_input, -1)) / CHANNEL_COUNT
    input_gradient = gradient_float + inverse_deviation[..., None] * (gradient_centered - first_term[..., None] - centered_input * second_term[..., None])
    return (input_gradient.astype(jnp.bfloat16), (dw_in, dw_out, db_in, gain_gradient, dshift))

def reference(patches, cotangent, w_token_in, b_token_in, w_token_out, layer_norm_gain, layer_norm_bias):
    xs = patches.reshape(N_DP, IMG_DEV, P_SIZE, CHANNEL_COUNT)
    gs = cotangent.reshape(N_DP, IMG_DEV, P_SIZE, CHANNEL_COUNT)

    def step(carry, pair):
        input_gradient, parts = block_grads(pair[0], pair[1], w_token_in, b_token_in, w_token_out, layer_norm_gain, layer_norm_bias)
        return (jax.tree.map(lambda a, b: a + b, carry, parts), input_gradient)
    init = (jnp.zeros((HID, P_SIZE), jnp.float32), jnp.zeros((P_SIZE, HID), jnp.float32), jnp.zeros((HID,), jnp.float32), jnp.zeros((CHANNEL_COUNT,), jnp.float32), jnp.zeros((CHANNEL_COUNT,), jnp.float32))
    totals, dxs = lax.scan(step, init, (xs, gs))
    images = float(IMAGES)
    return (dxs.reshape(IMAGES, P_SIZE, CHANNEL_COUNT), totals[0] / images, totals[1] / images, totals[2] / images, totals[3] / images, totals[4] / images)
```

```python
import functools
import math

import jax
import jax.numpy as jnp
from jax import lax
from jax.experimental import pallas as pl
from jax.experimental.pallas import tpu as pltpu
from jax.sharding import PartitionSpec as P


eps_norm = 1e-05
EXTRA = 16
F32 = jnp.float32
BF16 = jnp.bfloat16
VM = pl.BlockSpec(memory_space=pltpu.VMEM)


def call(body, outs, args, flops=0, name=None):
    nbytes = sum(a.size * a.dtype.itemsize for a in (*args, *outs))
    return pl.pallas_call(
        body,
        out_shape=outs,
        in_specs=[VM] * len(args),
        out_specs=[VM] * len(outs),
        name=name,
        cost_estimate=pl.CostEstimate(
            flops=flops, bytes_accessed=nbytes, transcendentals=0
        ),
    )(*args)


def shape(dims, dtype=F32):
    return jax.ShapeDtypeStruct(tuple(dims), dtype)


def dot(a, b, ca, cb, precision=None):
    return lax.dot_general(
        a, b, (((ca,), (cb,)), ((), ())), precision=precision, preferred_element_type=F32
    )


def high_low(v):
    high = v.astype(BF16)
    return high, (v - high.astype(F32)).astype(BF16)


def tree(values):
    values = list(values)
    while len(values) > 1:
        values = [a + b for a, b in zip(values[::2], values[1::2], strict=True)]
    return values[0]


def radices_of(n):
    factors, left = [2], n // 2
    while left > 1:
        r = 4 if left % 4 == 0 else 2
        factors.append(r)
        left //= r
    assert math.prod(factors) == n
    return factors


def exchange(value, axis, n, stride, radix):
    return [
        lax.ppermute(value, axis, [(i, i ^ (j * stride)) for i in range(n)])
        for j in range(1, radix)
    ]


def exchange_each(values, axis, n, stride):
    return [
        lax.ppermute(v, axis, [(i, i ^ (j * stride)) for i in range(n)])
        for j, v in enumerate(values, 1)
    ]


def tiny_rows(row, extra=EXTRA):
    high, low = high_low(row)
    return jnp.concatenate([high, low, jnp.zeros((extra - 2, row.shape[1]), BF16)], axis=0)


def join_pair(block):
    return block[0:1].astype(F32) + block[1:2].astype(F32)


def stats_body(x_ref, o_ref):
    images = x_ref.shape[0]
    for b in range(images):
        x = x_ref[b].astype(F32)
        o_ref[b : b + 1, :] = jnp.sum(x, axis=0, keepdims=True)
        o_ref[images + b : images + b + 1, :] = jnp.sum(x * x, axis=0, keepdims=True)


def early_body(n_chan, cot_ref, w_ref, gain_ref, bias_ref, ga_ref, gain_o, bias_o):
    images, width, patches = cot_ref.shape
    where = lax.axis_index("chan")
    for i in range(n_chan):

        @pl.when(where == i)
        def _():
            for src, dst in ((gain_ref, gain_o), (bias_ref, bias_o)):
                row = src[0:1, i * width : (i + 1) * width]
                rows = jnp.broadcast_to(row, (patches, width))
                dst[...] = jnp.transpose(rows, (1, 0))

    def image(b, carry):
        ga_ref[b] = dot(cot_ref[b], w_ref[...], 1, 0)
        return carry

    lax.fori_loop(0, images, image, 0)


def main_body(
    n_parts, channels, x_ref, *refs
):
    parts = refs[:n_parts]
    gain_ref, bias_ref, w_ref, b_ref, ga_ref = refs[n_parts : n_parts + 5]
    mr_ref, n_ref, act_ref, gp_ref, db_ref, pre_ref, acc_ref = refs[n_parts + 5 :]
    images, width, patches = x_ref.shape
    hidden = w_ref.shape[0]
    totals = tree([p[...] for p in parts]) / channels
    mean = totals[:images]
    rstd = lax.rsqrt(totals[images:] - mean * mean + eps_norm)
    mr_ref[0] = mean
    mr_ref[1] = rstd
    acc_ref[...] = jnp.zeros_like(acc_ref)
    step = 32

    def image(b, carry):
        xhat = (x_ref[b].astype(F32) - mr_ref[0, pl.ds(b, 1), :]) * mr_ref[1, pl.ds(b, 1), :]
        normed = (xhat * gain_ref[...] + bias_ref[...]).astype(BF16)
        n_ref[b] = normed
        pre_ref[...] = dot(normed, w_ref[...], 1, 1)
        for r in range(0, width, step):
            rows = pl.ds(r, step)
            pre = pre_ref[rows, :] + b_ref[...]
            cdf = 0.5 * (1.0 + lax.erf(pre * (1.0 / math.sqrt(2.0))))
            act_ref[b, rows, :] = (pre * cdf).astype(BF16)
            slope = cdf + pre * jnp.exp(-0.5 * pre * pre) * (1.0 / math.sqrt(2.0 * math.pi))
            gp = (ga_ref[b, rows, :] * slope).astype(BF16)
            gp_ref[b, rows, :] = gp
            gpf = gp.astype(F32)
            acc_ref[...] += functools.reduce(
                jnp.add, [gpf[i : i + 8] for i in range(0, step, 8)]
            )
        return carry

    lax.fori_loop(0, images, image, 0)
    db_ref[...] = jnp.sum(acc_ref[...], axis=0, keepdims=True)


def weight_dots(which, cot_ref, act_ref, n_ref, gp_ref, store):
    rows = cot_ref.shape[0] * cot_ref.shape[1]

    @pl.when(which == 0)
    def _():
        store(dot(flat(cot_ref, rows), flat(act_ref, rows), 0, 0))

    @pl.when(which != 0)
    def _():
        store(dot(flat(n_ref, rows), flat(gp_ref, rows), 0, 0))


def flat(ref, rows):
    return ref[...].reshape(rows, ref.shape[2])


def send_body(cot_ref, act_ref, n_ref, gp_ref, db_ref, o_ref):
    patches = cot_ref.shape[2]
    core = lax.rem(lax.axis_index("dp"), 2)

    def store(v):
        o_ref[0:patches, :] = v.astype(BF16)

    weight_dots(1 - core, cot_ref, act_ref, n_ref, gp_ref, store)
    o_ref[patches:, :] = tiny_rows(db_ref[...])


def keep_body(cot_ref, act_ref, n_ref, gp_ref, o_ref):
    core = lax.rem(lax.axis_index("dp"), 2)

    def store(v):
        o_ref[...] = v

    weight_dots(core, cot_ref, act_ref, n_ref, gp_ref, store)


def scatter_body(radix, stride, n_got, own_ref, db_ref, *refs):
    got, (keep_ref, dbo_ref, *sends) = refs[:n_got], refs[n_got:]
    rows = own_ref.shape[0]
    chunk = rows // radix
    me = lax.rem(lax.axis_index("dp") // stride, radix)
    db = tree([join_pair(tiny_rows(db_ref[...]))] + [join_pair(g[rows:, :]) for g in got])
    dbo_ref[...] = db
    tiny = tiny_rows(db)
    for i in range(radix):
        span = slice(i * chunk, (i + 1) * chunk)
        part = own_ref[span, :]
        for g in got:
            part = part + g[span, :].astype(F32)

        @pl.when(me == i)
        def _():
            keep_ref[...] = part

        for j, send in enumerate(sends, 1):

            @pl.when(me == i ^ j)
            def _():
                send[0:chunk, :] = part.astype(BF16)

    for send in sends:
        send[chunk:, :] = tiny


def norm_body(scale_dummy, x_ref, mr_ref, gain_ref, gp_ref, w_ref, gn_ref, sums_ref, norm_ref, acc_ref):
    images, width, patches = x_ref.shape
    acc_ref[...] = jnp.zeros_like(acc_ref)

    def image(b, carry):
        gn = dot(gp_ref[b], w_ref[...], 1, 0).astype(BF16)
        gn_ref[b] = gn
        gnf = gn.astype(F32)
        xhat = (x_ref[b].astype(F32) - mr_ref[0, pl.ds(b, 1), :]) * mr_ref[1, pl.ds(b, 1), :]
        prod = gnf * xhat
        acc_ref[0] += prod
        acc_ref[1] += gnf
        gain = gain_ref[...]
        sums_ref[pl.ds(b, 1), :] = jnp.sum(gnf * gain, axis=0, keepdims=True)
        sums_ref[pl.ds(images + b, 1), :] = jnp.sum(prod * gain, axis=0, keepdims=True)
        return carry

    lax.fori_loop(0, images, image, 0)
    ones = jnp.ones((8, patches), F32)
    norm_ref[...] = jnp.zeros_like(norm_ref)
    for i in range(2):
        row = dot(ones, acc_ref[i], 1, 1, precision=lax.Precision.HIGHEST)
        norm_ref[0:1, i * width : (i + 1) * width] = row[0:1]


def pack_body(n_got, own_ref, db_ref, sums_ref, *refs):
    got, (o_ref,) = refs[:n_got], refs[n_got:]
    rows, hidden = own_ref.shape
    total = own_ref[...]
    for g in got:
        total = total + g[0:rows, :].astype(F32)
    o_ref[0:rows, :] = total.astype(BF16)
    db = tree([join_pair(tiny_rows(db_ref[...]))] + [join_pair(g[rows:, :]) for g in got])
    o_ref[rows : rows + EXTRA, :] = tiny_rows(db)
    n, patches = sums_ref.shape
    high, low = high_low(sums_ref[...])
    o_ref[rows + EXTRA :, :] = jnp.zeros((n, hidden), BF16)
    o_ref[rows + EXTRA :, 0:patches] = high
    o_ref[rows + EXTRA :, patches : 2 * patches] = low


def total_body(n_got, scale, channels, mine_ref, norm_ref, *refs):
    got, (o_ref, db_ref, terms_ref) = refs[:n_got], refs[n_got:]
    n, patches = terms_ref.shape
    rows = mine_ref.shape[0] - EXTRA - n
    every = (mine_ref, *got)
    o_ref[0:rows, :] = (tree([r[0:rows, :].astype(F32) for r in every]) * scale).astype(BF16)
    o_ref[rows:, :] = tiny_rows(norm_ref[...])
    db_ref[...] = tree([join_pair(r[rows : rows + EXTRA, :]) for r in every]) * scale
    sums = tree(
        [
            r[rows + EXTRA :, 0:patches].astype(F32)
            + r[rows + EXTRA :, patches : 2 * patches].astype(F32)
            for r in every
        ]
    )
    terms_ref[...] = sums / channels


def input_body(x_ref, cot_ref, gn_ref, mr_ref, gain_ref, terms_ref, o_ref):
    images = x_ref.shape[0]

    def image(b, carry):
        one = pl.ds(b, 1)
        mean, rstd = mr_ref[0, one, :], mr_ref[1, one, :]
        xhat = (x_ref[b].astype(F32) - mean) * rstd
        hat = gn_ref[b].astype(F32) * gain_ref[...]
        inner = hat - terms_ref[one, :] - xhat * terms_ref[pl.ds(images + b, 1), :]
        o_ref[b] = (cot_ref[b].astype(F32) + rstd * inner).astype(BF16)
        return carry

    lax.fori_loop(0, images, image, 0)


def gather_body(radix, stride, mine_ref, *refs):
    got, (o_ref,) = refs[:-1], refs[-1:]
    rows = mine_ref.shape[0] - EXTRA
    me = lax.rem(lax.axis_index("dp") // stride, radix)
    every = (mine_ref, *got)
    for j, r in enumerate(every):
        for i in range(radix):

            @pl.when(me == i ^ j)
            def _():
                o_ref[i * rows : (i + 1) * rows, :] = r[0:rows, :]

    o_ref[radix * rows :, :] = tiny_rows(tree([join_pair(r[rows:, :]) for r in every]))


def last_body(scale, mine_ref, got_ref, out_ref, in_ref, norm_ref):
    rows = mine_ref.shape[0] - EXTRA
    core = lax.rem(lax.axis_index("dp"), 2)
    norm_ref[...] = (join_pair(mine_ref[rows:, :]) + join_pair(got_ref[rows:, :])) * scale

    def finish(a_ref, b_ref):
        out_ref[...] = a_ref[0:rows, :].astype(F32)
        in_ref[...] = jnp.transpose(b_ref[0:rows, :].astype(F32), (1, 0))

    @pl.when(core == 0)
    def _():
        finish(mine_ref, got_ref)

    @pl.when(core != 0)
    def _():
        finish(got_ref, mine_ref)


def shards(
    patches, cotangent, w_token_in, b_token_in, w_token_out, layer_norm_gain, layer_norm_bias
):
    n_dp, n_chan = lax.axis_size("dp"), lax.axis_size("chan")
    channels = layer_norm_gain.shape[0]
    x, cot = jnp.swapaxes(patches, 1, 2), jnp.swapaxes(cotangent, 1, 2)
    images, width, n_patch = x.shape
    hidden = w_token_in.shape[0]
    scale = 1.0 / (images * n_dp)
    work = 2 * images * width * n_patch * hidden
    assert 2 * width <= hidden and 2 * n_patch <= hidden

    (sums,) = call(stats_body, [shape((2 * images, n_patch))], [x], name="stats")
    others = exchange(sums, "chan", n_chan, 1, n_chan)
    ga, gain, bias = call(
        functools.partial(early_body, n_chan),
        [shape((images, width, hidden)), shape((width, n_patch)), shape((width, n_patch))],
        [cot, w_token_out, layer_norm_gain[None], layer_norm_bias[None]],
        flops=work,
        name="early",
    )
    args = [x, sums, *others, gain, bias, w_token_in, b_token_in[None], ga]
    outs = [
        shape((2, images, n_patch)),
        shape(x.shape, BF16),
        shape((images, width, hidden), BF16),
        shape((images, width, hidden), BF16),
        shape((1, hidden)),
    ]
    mr, normed, act, gp, db = pl.pallas_call(
        functools.partial(main_body, n_chan, channels),
        out_shape=outs,
        in_specs=[VM] * len(args),
        out_specs=[VM] * len(outs),
        scratch_shapes=[pltpu.VMEM((width, hidden), F32), pltpu.VMEM((8, hidden), F32)],
        name="main",
    )(*args)

    quad = [cot, act, normed, gp]
    (send,) = call(
        send_body, [shape((n_patch + EXTRA, hidden), BF16)], [*quad, db], flops=work, name="send"
    )
    radices = radices_of(n_dp)
    got = exchange_each([send], "dp", n_dp, 1)
    (own,) = call(keep_body, [shape((n_patch, hidden))], quad, flops=work, name="keep")
    stride = radices[0]
    rows = n_patch
    for radix in radices[1:]:
        rows //= radix
        own, db, *sends = call(
            functools.partial(scatter_body, radix, stride, len(got)),
            [shape((rows, hidden)), shape((1, hidden))]
            + [shape((rows + EXTRA, hidden), BF16)] * (radix - 1),
            [own, db, *got],
            name="scatter",
        )
        got = exchange_each(sends, "dp", n_dp, stride)
        stride *= radix

    gn, sums, norm = pl.pallas_call(
        functools.partial(norm_body, None),
        out_shape=[shape(x.shape, BF16), shape((2 * images, n_patch)), shape((1, hidden))],
        in_specs=[VM] * 5,
        out_specs=[VM] * 3,
        scratch_shapes=[pltpu.VMEM((2, width, n_patch), F32)],
        name="norm",
        cost_estimate=pl.CostEstimate(flops=work, bytes_accessed=1 << 22, transcendentals=0),
    )(x, mr, gain, gp, w_token_in)

    (message,) = call(
        functools.partial(pack_body, len(got)),
        [shape((rows + EXTRA + 2 * images, hidden), BF16)],
        [own, db, sums, *got],
        name="pack",
    )
    others = exchange(message, "chan", n_chan, 1, n_chan)
    block, db, terms = call(
        functools.partial(total_body, len(others), scale, channels),
        [shape((rows + EXTRA, hidden), BF16), shape((1, hidden)), shape((2 * images, n_patch))],
        [message, norm, *others],
        name="total",
    )
    final = None
    for radix in radices[:0:-1]:
        stride //= radix
        got = exchange(block, "dp", n_dp, stride, radix)
        if final is None:
            (final,) = call(
                input_body, [shape(x.shape, BF16)], [x, cot, gn, mr, gain, terms], name="input"
            )
        rows *= radix
        (block,) = call(
            functools.partial(gather_body, radix, stride),
            [shape((rows + EXTRA, hidden), BF16)],
            [block, *got],
            name="gather",
        )
    (got,) = exchange(block, "dp", n_dp, 1, 2)
    dw_out, dw_in, norm = call(
        functools.partial(last_body, scale),
        [shape((n_patch, hidden)), shape((hidden, n_patch)), shape((1, hidden))],
        [block, got],
        name="last",
    )
    return (
        jnp.swapaxes(final, 1, 2),
        dw_in,
        dw_out,
        db[0],
        norm[0, 0:width],
        norm[0, width : 2 * width],
    )


def solution(mesh):
    placed = (P("dp", None, "chan"), P("dp", None, "chan"), P(), P(), P(), P(), P())
    return jax.shard_map(
        shards,
        mesh=mesh,
        in_specs=placed,
        out_specs=(P("dp", None, "chan"), P(), P(), P(), P("chan"), P("chan")),
        check_vma=False,
    )
```

```python
import functools
import math

import jax
import jax.numpy as jnp
from jax import lax
from jax.experimental import pallas as pl
from jax.experimental.pallas import tpu as pltpu
from jax.sharding import PartitionSpec as P


eps_norm = 1e-05
EXTRA = 16
F32 = jnp.float32
BF16 = jnp.bfloat16
VM = pl.BlockSpec(memory_space=pltpu.VMEM)
LIMIT = pltpu.CompilerParams(vmem_limit_bytes=24 << 20)


def call(body, outs, args, flops=0, name=None):
    nbytes = sum(a.size * a.dtype.itemsize for a in (*args, *outs))
    return pl.pallas_call(
        body,
        out_shape=outs,
        in_specs=[VM] * len(args),
        out_specs=[VM] * len(outs),
        name=name,
        compiler_params=LIMIT,
        cost_estimate=pl.CostEstimate(
            flops=flops, bytes_accessed=nbytes, transcendentals=0
        ),
    )(*args)


def shape(dims, dtype=F32):
    return jax.ShapeDtypeStruct(tuple(dims), dtype)


def dot(a, b, ca, cb, precision=None):
    return lax.dot_general(
        a, b, (((ca,), (cb,)), ((), ())), precision=precision, preferred_element_type=F32
    )


def high_low(v):
    high = v.astype(BF16)
    return high, (v - high.astype(F32)).astype(BF16)


def tree(values):
    values = list(values)
    while len(values) > 1:
        values = [a + b for a, b in zip(values[::2], values[1::2], strict=True)]
    return values[0]


def radices_of(n):
    factors, left = [2], n // 2
    while left > 1:
        r = 4 if left % 4 == 0 else 2
        factors.append(r)
        left //= r
    assert math.prod(factors) == n
    return factors


def exchange(value, axis, n, stride, radix):
    return [
        lax.ppermute(value, axis, [(i, i ^ (j * stride)) for i in range(n)])
        for j in range(1, radix)
    ]


def exchange_each(values, axis, n, stride):
    return [
        lax.ppermute(v, axis, [(i, i ^ (j * stride)) for i in range(n)])
        for j, v in enumerate(values, 1)
    ]


def tiny_rows(row, extra=EXTRA):
    high, low = high_low(row)
    return jnp.concatenate([high, low, jnp.zeros((extra - 2, row.shape[1]), BF16)], axis=0)


def join_pair(block):
    return block[0:1].astype(F32) + block[1:2].astype(F32)


def stats_body(x_ref, o_ref):
    images = x_ref.shape[0]
    for b in range(images):
        x = x_ref[b].astype(F32)
        o_ref[b : b + 1, :] = jnp.sum(x, axis=0, keepdims=True)
        o_ref[images + b : images + b + 1, :] = jnp.sum(x * x, axis=0, keepdims=True)


def early_body(n_chan, cot_ref, w_ref, gain_ref, bias_ref, ga_ref, gain_o, bias_o):
    images, width, patches = cot_ref.shape
    where = lax.axis_index("chan")
    for i in range(n_chan):

        @pl.when(where == i)
        def _():
            for src, dst in ((gain_ref, gain_o), (bias_ref, bias_o)):
                row = src[0:1, i * width : (i + 1) * width]
                rows = jnp.broadcast_to(row, (patches, width))
                dst[...] = jnp.transpose(rows, (1, 0))

    def image(b, carry):
        ga_ref[b] = dot(cot_ref[b], w_ref[...], 1, 0)
        return carry

    lax.fori_loop(0, images, image, 0)


def main_body(
    n_parts, channels, x_ref, *refs
):
    parts = refs[:n_parts]
    gain_ref, bias_ref, w_ref, b_ref, ga_ref = refs[n_parts : n_parts + 5]
    mr_ref, n_ref, act_ref, gp_ref, db_ref, pre_ref, acc_ref = refs[n_parts + 5 :]
    images, width, patches = x_ref.shape
    hidden = w_ref.shape[0]
    totals = tree([p[...] for p in parts]) / channels
    mean = totals[:images]
    rstd = lax.rsqrt(totals[images:] - mean * mean + eps_norm)
    mr_ref[0] = mean
    mr_ref[1] = rstd
    acc_ref[...] = jnp.zeros_like(acc_ref)
    step = 32

    def image(b, carry):
        xhat = (x_ref[b].astype(F32) - mr_ref[0, pl.ds(b, 1), :]) * mr_ref[1, pl.ds(b, 1), :]
        normed = (xhat * gain_ref[...] + bias_ref[...]).astype(BF16)
        n_ref[b] = normed
        pre_ref[...] = dot(normed, w_ref[...], 1, 1)
        for r in range(0, width, step):
            rows = pl.ds(r, step)
            pre = pre_ref[rows, :] + b_ref[...]
            cdf = 0.5 * (1.0 + lax.erf(pre * (1.0 / math.sqrt(2.0))))
            act_ref[b, rows, :] = (pre * cdf).astype(BF16)
            slope = cdf + pre * jnp.exp(-0.5 * pre * pre) * (1.0 / math.sqrt(2.0 * math.pi))
            gp = (ga_ref[b, rows, :] * slope).astype(BF16)
            gp_ref[b, rows, :] = gp
            gpf = gp.astype(F32)
            acc_ref[...] += functools.reduce(
                jnp.add, [gpf[i : i + 8] for i in range(0, step, 8)]
            )
        return carry

    lax.fori_loop(0, images, image, 0)
    db_ref[...] = jnp.sum(acc_ref[...], axis=0, keepdims=True)


def weight_dots(which, cot_ref, act_ref, n_ref, gp_ref, store):
    rows = cot_ref.shape[0] * cot_ref.shape[1]

    @pl.when(which == 0)
    def _():
        store(dot(flat(cot_ref, rows), flat(act_ref, rows), 0, 0))

    @pl.when(which != 0)
    def _():
        store(dot(flat(n_ref, rows), flat(gp_ref, rows), 0, 0))


def flat(ref, rows):
    return ref[...].reshape(rows, ref.shape[2])


def send_body(cot_ref, act_ref, n_ref, gp_ref, db_ref, o_ref):
    patches = cot_ref.shape[2]
    core = lax.rem(lax.axis_index("dp"), 2)

    def store(v):
        o_ref[0:patches, :] = v.astype(BF16)

    weight_dots(1 - core, cot_ref, act_ref, n_ref, gp_ref, store)
    o_ref[patches:, :] = tiny_rows(db_ref[...])


def keep_body(cot_ref, act_ref, n_ref, gp_ref, o_ref):
    core = lax.rem(lax.axis_index("dp"), 2)

    def store(v):
        o_ref[...] = v

    weight_dots(core, cot_ref, act_ref, n_ref, gp_ref, store)


def scatter_body(radix, stride, n_got, own_ref, db_ref, *refs):
    got, (keep_ref, dbo_ref, *sends) = refs[:n_got], refs[n_got:]
    rows = own_ref.shape[0]
    chunk = rows // radix
    me = lax.rem(lax.axis_index("dp") // stride, radix)
    db = tree([join_pair(tiny_rows(db_ref[...]))] + [join_pair(g[rows:, :]) for g in got])
    dbo_ref[...] = db
    tiny = tiny_rows(db)
    for i in range(radix):
        span = slice(i * chunk, (i + 1) * chunk)
        part = own_ref[span, :]
        for g in got:
            part = part + g[span, :].astype(F32)

        @pl.when(me == i)
        def _():
            keep_ref[...] = part

        for j, send in enumerate(sends, 1):

            @pl.when(me == i ^ j)
            def _():
                send[0:chunk, :] = part.astype(BF16)

    for send in sends:
        send[chunk:, :] = tiny


def norm_body(scale_dummy, x_ref, mr_ref, gain_ref, gp_ref, w_ref, gn_ref, sums_ref, norm_ref, acc_ref):
    images, width, patches = x_ref.shape
    acc_ref[...] = jnp.zeros_like(acc_ref)

    def image(b, carry):
        gn = dot(gp_ref[b], w_ref[...], 1, 0).astype(BF16)
        gn_ref[b] = gn
        gnf = gn.astype(F32)
        xhat = (x_ref[b].astype(F32) - mr_ref[0, pl.ds(b, 1), :]) * mr_ref[1, pl.ds(b, 1), :]
        prod = gnf * xhat
        acc_ref[0] += prod
        acc_ref[1] += gnf
        gain = gain_ref[...]
        sums_ref[pl.ds(b, 1), :] = jnp.sum(gnf * gain, axis=0, keepdims=True)
        sums_ref[pl.ds(images + b, 1), :] = jnp.sum(prod * gain, axis=0, keepdims=True)
        return carry

    lax.fori_loop(0, images, image, 0)
    ones = jnp.ones((8, patches), F32)
    norm_ref[...] = jnp.zeros_like(norm_ref)
    for i in range(2):
        row = dot(ones, acc_ref[i], 1, 1, precision=lax.Precision.HIGHEST)
        norm_ref[0:1, i * width : (i + 1) * width] = row[0:1]


def pack_body(n_got, own_ref, db_ref, sums_ref, *refs):
    got, (o_ref,) = refs[:n_got], refs[n_got:]
    rows, hidden = own_ref.shape
    total = own_ref[...]
    for g in got:
        total = total + g[0:rows, :].astype(F32)
    o_ref[0:rows, :] = total.astype(BF16)
    db = tree([join_pair(tiny_rows(db_ref[...]))] + [join_pair(g[rows:, :]) for g in got])
    o_ref[rows : rows + EXTRA, :] = tiny_rows(db)
    n, patches = sums_ref.shape
    high, low = high_low(sums_ref[...])
    o_ref[rows + EXTRA :, :] = jnp.zeros((n, hidden), BF16)
    o_ref[rows + EXTRA :, 0:patches] = high
    o_ref[rows + EXTRA :, patches : 2 * patches] = low


def total_body(n_got, scale, channels, mine_ref, norm_ref, *refs):
    got, (o_ref, db_ref, terms_ref) = refs[:n_got], refs[n_got:]
    n, patches = terms_ref.shape
    rows = mine_ref.shape[0] - EXTRA - n
    every = (mine_ref, *got)
    o_ref[0:rows, :] = (tree([r[0:rows, :].astype(F32) for r in every]) * scale).astype(BF16)
    o_ref[rows:, :] = tiny_rows(norm_ref[...])
    db_ref[...] = tree([join_pair(r[rows : rows + EXTRA, :]) for r in every]) * scale
    sums = tree(
        [
            r[rows + EXTRA :, 0:patches].astype(F32)
            + r[rows + EXTRA :, patches : 2 * patches].astype(F32)
            for r in every
        ]
    )
    terms_ref[...] = sums / channels


def input_body(x_ref, cot_ref, gn_ref, mr_ref, gain_ref, terms_ref, o_ref):
    images = x_ref.shape[0]

    def image(b, carry):
        one = pl.ds(b, 1)
        mean, rstd = mr_ref[0, one, :], mr_ref[1, one, :]
        xhat = (x_ref[b].astype(F32) - mean) * rstd
        hat = gn_ref[b].astype(F32) * gain_ref[...]
        inner = hat - terms_ref[one, :] - xhat * terms_ref[pl.ds(images + b, 1), :]
        o_ref[b] = (cot_ref[b].astype(F32) + rstd * inner).astype(BF16)
        return carry

    lax.fori_loop(0, images, image, 0)


def gather_body(radix, stride, mine_ref, *refs):
    got, (o_ref,) = refs[:-1], refs[-1:]
    rows = mine_ref.shape[0] - EXTRA
    me = lax.rem(lax.axis_index("dp") // stride, radix)
    every = (mine_ref, *got)
    for j, r in enumerate(every):
        for i in range(radix):

            @pl.when(me == i ^ j)
            def _():
                o_ref[i * rows : (i + 1) * rows, :] = r[0:rows, :]

    o_ref[radix * rows :, :] = tiny_rows(tree([join_pair(r[rows:, :]) for r in every]))


def last_body(scale, mine_ref, got_ref, out_ref, in_ref, norm_ref):
    rows = mine_ref.shape[0] - EXTRA
    core = lax.rem(lax.axis_index("dp"), 2)
    norm_ref[...] = (join_pair(mine_ref[rows:, :]) + join_pair(got_ref[rows:, :])) * scale

    def finish(a_ref, b_ref):
        out_ref[...] = a_ref[0:rows, :].astype(F32)
        in_ref[...] = jnp.transpose(b_ref[0:rows, :].astype(F32), (1, 0))

    @pl.when(core == 0)
    def _():
        finish(mine_ref, got_ref)

    @pl.when(core != 0)
    def _():
        finish(got_ref, mine_ref)


def shards(
    patches, cotangent, w_token_in, b_token_in, w_token_out, layer_norm_gain, layer_norm_bias
):
    n_dp, n_chan = lax.axis_size("dp"), lax.axis_size("chan")
    channels = layer_norm_gain.shape[0]
    x, cot = jnp.swapaxes(patches, 1, 2), jnp.swapaxes(cotangent, 1, 2)
    images, width, n_patch = x.shape
    hidden = w_token_in.shape[0]
    scale = 1.0 / (images * n_dp)
    work = 2 * images * width * n_patch * hidden
    assert 2 * width <= hidden and 2 * n_patch <= hidden

    (sums,) = call(stats_body, [shape((2 * images, n_patch))], [x], name="stats")
    others = exchange(sums, "chan", n_chan, 1, n_chan)
    ga, gain, bias = call(
        functools.partial(early_body, n_chan),
        [shape((images, width, hidden)), shape((width, n_patch)), shape((width, n_patch))],
        [cot, w_token_out, layer_norm_gain[None], layer_norm_bias[None]],
        flops=work,
        name="early",
    )
    args = [x, sums, *others, gain, bias, w_token_in, b_token_in[None], ga]
    outs = [
        shape((2, images, n_patch)),
        shape(x.shape, BF16),
        shape((images, width, hidden), BF16),
        shape((images, width, hidden), BF16),
        shape((1, hidden)),
    ]
    mr, normed, act, gp, db = pl.pallas_call(
        functools.partial(main_body, n_chan, channels),
        out_shape=outs,
        in_specs=[VM] * len(args),
        out_specs=[VM] * len(outs),
        scratch_shapes=[pltpu.VMEM((width, hidden), F32), pltpu.VMEM((8, hidden), F32)],
        name="main",
        compiler_params=LIMIT,
    )(*args)

    quad = [cot, act, normed, gp]
    (send,) = call(
        send_body, [shape((n_patch + EXTRA, hidden), BF16)], [*quad, db], flops=work, name="send"
    )
    radices = radices_of(n_dp)
    got = exchange_each([send], "dp", n_dp, 1)
    (own,) = call(keep_body, [shape((n_patch, hidden))], quad, flops=work, name="keep")
    stride = radices[0]
    rows = n_patch
    for radix in radices[1:]:
        rows //= radix
        own, db, *sends = call(
            functools.partial(scatter_body, radix, stride, len(got)),
            [shape((rows, hidden)), shape((1, hidden))]
            + [shape((rows + EXTRA, hidden), BF16)] * (radix - 1),
            [own, db, *got],
            name="scatter",
        )
        got = exchange_each(sends, "dp", n_dp, stride)
        stride *= radix

    gn, sums, norm = pl.pallas_call(
        functools.partial(norm_body, None),
        out_shape=[shape(x.shape, BF16), shape((2 * images, n_patch)), shape((1, hidden))],
        in_specs=[VM] * 5,
        out_specs=[VM] * 3,
        scratch_shapes=[pltpu.VMEM((2, width, n_patch), F32)],
        name="norm",
        compiler_params=LIMIT,
        cost_estimate=pl.CostEstimate(flops=work, bytes_accessed=1 << 22, transcendentals=0),
    )(x, mr, gain, gp, w_token_in)

    (message,) = call(
        functools.partial(pack_body, len(got)),
        [shape((rows + EXTRA + 2 * images, hidden), BF16)],
        [own, db, sums, *got],
        name="pack",
    )
    others = exchange(message, "chan", n_chan, 1, n_chan)
    block, db, terms = call(
        functools.partial(total_body, len(others), scale, channels),
        [shape((rows + EXTRA, hidden), BF16), shape((1, hidden)), shape((2 * images, n_patch))],
        [message, norm, *others],
        name="total",
    )
    final = None
    for radix in radices[:0:-1]:
        stride //= radix
        got = exchange(block, "dp", n_dp, stride, radix)
        if final is None:
            (final,) = call(
                input_body, [shape(x.shape, BF16)], [x, cot, gn, mr, gain, terms], name="input"
            )
        rows *= radix
        (block,) = call(
            functools.partial(gather_body, radix, stride),
            [shape((rows + EXTRA, hidden), BF16)],
            [block, *got],
            name="gather",
        )
    (got,) = exchange(block, "dp", n_dp, 1, 2)
    dw_out, dw_in, norm = call(
        functools.partial(last_body, scale),
        [shape((n_patch, hidden)), shape((hidden, n_patch)), shape((1, hidden))],
        [block, got],
        name="last",
    )
    return (
        jnp.swapaxes(final, 1, 2),
        dw_in,
        dw_out,
        db[0],
        norm[0, 0:width],
        norm[0, width : 2 * width],
    )


def solution(mesh):
    placed = (P("dp", None, "chan"), P("dp", None, "chan"), P(), P(), P(), P(), P())
    return jax.shard_map(
        shards,
        mesh=mesh,
        in_specs=placed,
        out_specs=(P("dp", None, "chan"), P(), P(), P(), P("chan"), P("chan")),
        check_vma=False,
    )
```

```python
import functools
import math

import jax
import jax.numpy as jnp
from jax import lax
from jax.experimental import pallas as pl
from jax.experimental.pallas import tpu as pltpu
from jax.sharding import PartitionSpec as P


eps_norm = 1e-05
EXTRA = 16
F32 = jnp.float32
BF16 = jnp.bfloat16
VM = pl.BlockSpec(memory_space=pltpu.VMEM)
LIMIT = pltpu.CompilerParams(vmem_limit_bytes=24 << 20)


def call(body, outs, args, flops=0, name=None):
    nbytes = sum(a.size * a.dtype.itemsize for a in (*args, *outs))
    return pl.pallas_call(
        body,
        out_shape=outs,
        in_specs=[VM] * len(args),
        out_specs=[VM] * len(outs),
        name=name,
        compiler_params=LIMIT,
        cost_estimate=pl.CostEstimate(
            flops=flops, bytes_accessed=nbytes, transcendentals=0
        ),
    )(*args)


def shape(dims, dtype=F32):
    return jax.ShapeDtypeStruct(tuple(dims), dtype)


def dot(a, b, ca, cb, precision=None):
    return lax.dot_general(
        a, b, (((ca,), (cb,)), ((), ())), precision=precision, preferred_element_type=F32
    )


def high_low(v):
    high = v.astype(BF16)
    return high, (v - high.astype(F32)).astype(BF16)


def tree(values):
    values = list(values)
    while len(values) > 1:
        values = [a + b for a, b in zip(values[::2], values[1::2], strict=True)]
    return values[0]


def radices_of(n):
    factors, left = [2], n // 2
    while left > 1:
        r = 4 if left % 4 == 0 else 2
        factors.append(r)
        left //= r
    assert math.prod(factors) == n
    return factors


def exchange(value, axis, n, stride, radix):
    return [
        lax.ppermute(value, axis, [(i, i ^ (j * stride)) for i in range(n)])
        for j in range(1, radix)
    ]


def exchange_each(values, axis, n, stride):
    return [
        lax.ppermute(v, axis, [(i, i ^ (j * stride)) for i in range(n)])
        for j, v in enumerate(values, 1)
    ]


def tiny_rows(row, extra=EXTRA):
    high, low = high_low(row)
    return jnp.concatenate([high, low, jnp.zeros((extra - 2, row.shape[1]), BF16)], axis=0)


def join_pair(block):
    return block[0:1].astype(F32) + block[1:2].astype(F32)


def stats_body(x_ref, o_ref):
    images = x_ref.shape[0]
    for b in range(images):
        x = x_ref[b].astype(F32)
        o_ref[b : b + 1, :] = jnp.sum(x, axis=0, keepdims=True)
        o_ref[images + b : images + b + 1, :] = jnp.sum(x * x, axis=0, keepdims=True)


def early_body(n_chan, cot_ref, w_ref, gain_ref, bias_ref, ga_ref, gain_o, bias_o):
    images, width, patches = cot_ref.shape
    where = lax.axis_index("chan")
    for i in range(n_chan):

        @pl.when(where == i)
        def _():
            for src, dst in ((gain_ref, gain_o), (bias_ref, bias_o)):
                row = src[0:1, i * width : (i + 1) * width]
                rows = jnp.broadcast_to(row, (patches, width))
                dst[...] = jnp.transpose(rows, (1, 0))

    def image(b, carry):
        ga_ref[b] = dot(cot_ref[b], w_ref[...], 1, 0)
        return carry

    lax.fori_loop(0, images, image, 0)


def main_body(
    n_parts, channels, x_ref, *refs
):
    parts = refs[:n_parts]
    gain_ref, bias_ref, w_ref, b_ref, ga_ref = refs[n_parts : n_parts + 5]
    mr_ref, n_ref, act_ref, gp_ref, db_ref, pre_ref, acc_ref = refs[n_parts + 5 :]
    images, width, patches = x_ref.shape
    hidden = w_ref.shape[0]
    totals = tree([p[...] for p in parts]) / channels
    mean = totals[:images]
    rstd = lax.rsqrt(totals[images:] - mean * mean + eps_norm)
    mr_ref[0] = mean
    mr_ref[1] = rstd
    acc_ref[...] = jnp.zeros_like(acc_ref)
    step = 32

    def image(b, carry):
        xhat = (x_ref[b].astype(F32) - mr_ref[0, pl.ds(b, 1), :]) * mr_ref[1, pl.ds(b, 1), :]
        normed = (xhat * gain_ref[...] + bias_ref[...]).astype(BF16)
        n_ref[b] = normed
        pre_ref[...] = dot(normed, w_ref[...], 1, 1)
        for r in range(0, width, step):
            rows = pl.ds(r, step)
            pre = pre_ref[rows, :] + b_ref[...]
            cdf = 0.5 * (1.0 + lax.erf(pre * (1.0 / math.sqrt(2.0))))
            act_ref[b, rows, :] = (pre * cdf).astype(BF16)
            slope = cdf + pre * jnp.exp(-0.5 * pre * pre) * (1.0 / math.sqrt(2.0 * math.pi))
            gp = (ga_ref[b, rows, :] * slope).astype(BF16)
            gp_ref[b, rows, :] = gp
            gpf = gp.astype(F32)
            acc_ref[...] += functools.reduce(
                jnp.add, [gpf[i : i + 8] for i in range(0, step, 8)]
            )
        return carry

    lax.fori_loop(0, images, image, 0)
    db_ref[...] = jnp.sum(acc_ref[...], axis=0, keepdims=True)


def weight_dots(which, cot_ref, act_ref, n_ref, gp_ref, store):
    rows = cot_ref.shape[0] * cot_ref.shape[1]

    @pl.when(which == 0)
    def _():
        store(dot(flat(cot_ref, rows), flat(act_ref, rows), 0, 0))

    @pl.when(which != 0)
    def _():
        store(dot(flat(n_ref, rows), flat(gp_ref, rows), 0, 0))


def flat(ref, rows):
    return ref[...].reshape(rows, ref.shape[2])


def send_body(cot_ref, act_ref, n_ref, gp_ref, db_ref, o_ref):
    patches = cot_ref.shape[2]
    core = lax.rem(lax.axis_index("dp"), 2)

    def store(v):
        o_ref[0:patches, :] = v.astype(BF16)

    weight_dots(1 - core, cot_ref, act_ref, n_ref, gp_ref, store)
    o_ref[patches:, :] = tiny_rows(db_ref[...])


def keep_body(cot_ref, act_ref, n_ref, gp_ref, o_ref):
    core = lax.rem(lax.axis_index("dp"), 2)

    def store(v):
        o_ref[...] = v

    weight_dots(core, cot_ref, act_ref, n_ref, gp_ref, store)


def scatter_body(radix, stride, n_got, own_ref, db_ref, *refs):
    got, (keep_ref, dbo_ref, *sends) = refs[:n_got], refs[n_got:]
    rows = own_ref.shape[0]
    chunk = rows // radix
    me = lax.rem(lax.axis_index("dp") // stride, radix)
    db = tree([join_pair(tiny_rows(db_ref[...]))] + [join_pair(g[rows:, :]) for g in got])
    dbo_ref[...] = db
    tiny = tiny_rows(db)
    for i in range(radix):
        span = slice(i * chunk, (i + 1) * chunk)
        part = own_ref[span, :]
        for g in got:
            part = part + g[span, :].astype(F32)

        @pl.when(me == i)
        def _():
            keep_ref[...] = part

        for j, send in enumerate(sends, 1):

            @pl.when(me == i ^ j)
            def _():
                send[0:chunk, :] = part.astype(BF16)

    for send in sends:
        send[chunk:, :] = tiny


def norm_body(scale_dummy, x_ref, mr_ref, gain_ref, gp_ref, w_ref, gn_ref, sums_ref, norm_ref, acc_ref):
    images, width, patches = x_ref.shape
    acc_ref[...] = jnp.zeros_like(acc_ref)

    def image(b, carry):
        gn = dot(gp_ref[b], w_ref[...], 1, 0).astype(BF16)
        gn_ref[b] = gn
        gnf = gn.astype(F32)
        xhat = (x_ref[b].astype(F32) - mr_ref[0, pl.ds(b, 1), :]) * mr_ref[1, pl.ds(b, 1), :]
        prod = gnf * xhat
        acc_ref[0] += prod
        acc_ref[1] += gnf
        gain = gain_ref[...]
        sums_ref[pl.ds(b, 1), :] = jnp.sum(gnf * gain, axis=0, keepdims=True)
        sums_ref[pl.ds(images + b, 1), :] = jnp.sum(prod * gain, axis=0, keepdims=True)
        return carry

    lax.fori_loop(0, images, image, 0)
    ones = jnp.ones((8, patches), F32)
    norm_ref[...] = jnp.zeros_like(norm_ref)
    for i in range(2):
        row = dot(ones, acc_ref[i], 1, 1, precision=lax.Precision.HIGHEST)
        norm_ref[0:1, i * width : (i + 1) * width] = row[0:1]


def pack_body(n_got, own_ref, db_ref, sums_ref, *refs):
    got, (o_ref,) = refs[:n_got], refs[n_got:]
    rows, hidden = own_ref.shape
    total = own_ref[...]
    for g in got:
        total = total + g[0:rows, :].astype(F32)
    o_ref[0:rows, :] = total.astype(BF16)
    db = tree([join_pair(tiny_rows(db_ref[...]))] + [join_pair(g[rows:, :]) for g in got])
    o_ref[rows : rows + EXTRA, :] = tiny_rows(db)
    n, patches = sums_ref.shape
    high, low = high_low(sums_ref[...])
    o_ref[rows + EXTRA :, :] = jnp.zeros((n, hidden), BF16)
    o_ref[rows + EXTRA :, 0:patches] = high
    o_ref[rows + EXTRA :, patches : 2 * patches] = low


def total_body(n_got, scale, channels, mine_ref, norm_ref, *refs):
    got, (o_ref, db_ref, terms_ref) = refs[:n_got], refs[n_got:]
    n, patches = terms_ref.shape
    rows = mine_ref.shape[0] - EXTRA - n
    every = (mine_ref, *got)
    o_ref[0:rows, :] = (tree([r[0:rows, :].astype(F32) for r in every]) * scale).astype(BF16)
    o_ref[rows:, :] = tiny_rows(norm_ref[...])
    db_ref[...] = tree([join_pair(r[rows : rows + EXTRA, :]) for r in every]) * scale
    sums = tree(
        [
            r[rows + EXTRA :, 0:patches].astype(F32)
            + r[rows + EXTRA :, patches : 2 * patches].astype(F32)
            for r in every
        ]
    )
    terms_ref[...] = sums / channels


def input_body(x_ref, cot_ref, gn_ref, mr_ref, gain_ref, terms_ref, o_ref):
    images = x_ref.shape[0]

    def image(b, carry):
        one = pl.ds(b, 1)
        mean, rstd = mr_ref[0, one, :], mr_ref[1, one, :]
        xhat = (x_ref[b].astype(F32) - mean) * rstd
        hat = gn_ref[b].astype(F32) * gain_ref[...]
        inner = hat - terms_ref[one, :] - xhat * terms_ref[pl.ds(images + b, 1), :]
        o_ref[b] = (cot_ref[b].astype(F32) + rstd * inner).astype(BF16)
        return carry

    lax.fori_loop(0, images, image, 0)


def gather_body(radix, stride, mine_ref, *refs):
    got, (o_ref,) = refs[:-1], refs[-1:]
    rows = mine_ref.shape[0] - EXTRA
    me = lax.rem(lax.axis_index("dp") // stride, radix)
    every = (mine_ref, *got)
    for j, r in enumerate(every):
        for i in range(radix):

            @pl.when(me == i ^ j)
            def _():
                o_ref[i * rows : (i + 1) * rows, :] = r[0:rows, :]

    o_ref[radix * rows :, :] = tiny_rows(tree([join_pair(r[rows:, :]) for r in every]))


def last_body(scale, mine_ref, got_ref, out_ref, in_ref, norm_ref):
    rows = mine_ref.shape[0] - EXTRA
    core = lax.rem(lax.axis_index("dp"), 2)
    norm_ref[...] = (join_pair(mine_ref[rows:, :]) + join_pair(got_ref[rows:, :])) * scale

    def finish(a_ref, b_ref):
        out_ref[...] = a_ref[0:rows, :].astype(F32)
        in_ref[...] = jnp.transpose(b_ref[0:rows, :].astype(F32), (1, 0))

    @pl.when(core == 0)
    def _():
        finish(mine_ref, got_ref)

    @pl.when(core != 0)
    def _():
        finish(got_ref, mine_ref)


def norm_call(x, mr, gain, gp, w_token_in, work):
    images, width, n_patch = x.shape
    hidden = gp.shape[2]
    return pl.pallas_call(
        functools.partial(norm_body, None),
        out_shape=[shape(x.shape, BF16), shape((2 * images, n_patch)), shape((1, hidden))],
        in_specs=[VM] * 5,
        out_specs=[VM] * 3,
        scratch_shapes=[pltpu.VMEM((2, width, n_patch), F32)],
        name="norm",
        compiler_params=LIMIT,
        cost_estimate=pl.CostEstimate(flops=work, bytes_accessed=1 << 22, transcendentals=0),
    )(x, mr, gain, gp, w_token_in)


def plain_plan(x, cot, mr, normed, act, gp, db, gain, w_token_in, scale, channels):
    n_dp, n_chan = lax.axis_size("dp"), lax.axis_size("chan")
    images, width, n_patch = x.shape
    hidden = act.shape[2]
    work = 2 * images * width * n_patch * hidden
    quad = [cot, act, normed, gp]
    (send,) = call(
        send_body, [shape((n_patch + EXTRA, hidden), BF16)], [*quad, db], flops=work, name="send"
    )
    radices = radices_of(n_dp)
    got = exchange_each([send], "dp", n_dp, 1)
    (own,) = call(keep_body, [shape((n_patch, hidden))], quad, flops=work, name="keep")
    stride = radices[0]
    rows = n_patch
    for radix in radices[1:]:
        rows //= radix
        own, db, *sends = call(
            functools.partial(scatter_body, radix, stride, len(got)),
            [shape((rows, hidden)), shape((1, hidden))]
            + [shape((rows + EXTRA, hidden), BF16)] * (radix - 1),
            [own, db, *got],
            name="scatter",
        )
        got = exchange_each(sends, "dp", n_dp, stride)
        stride *= radix

    gn, sums, norm = norm_call(x, mr, gain, gp, w_token_in, work)
    (message,) = call(
        functools.partial(pack_body, len(got)),
        [shape((rows + EXTRA + 2 * images, hidden), BF16)],
        [own, db, sums, *got],
        name="pack",
    )
    others = exchange(message, "chan", n_chan, 1, n_chan)
    block, db, terms = call(
        functools.partial(total_body, len(others), scale, channels),
        [shape((rows + EXTRA, hidden), BF16), shape((1, hidden)), shape((2 * images, n_patch))],
        [message, norm, *others],
        name="total",
    )
    final = None
    for radix in radices[:0:-1]:
        stride //= radix
        got = exchange(block, "dp", n_dp, stride, radix)
        if final is None:
            (final,) = call(
                input_body, [shape(x.shape, BF16)], [x, cot, gn, mr, gain, terms], name="input"
            )
        rows *= radix
        (block,) = call(
            functools.partial(gather_body, radix, stride),
            [shape((rows + EXTRA, hidden), BF16)],
            [block, *got],
            name="gather",
        )
    (got,) = exchange(block, "dp", n_dp, 1, 2)
    dw_out, dw_in, norm = call(
        functools.partial(last_body, scale),
        [shape((n_patch, hidden)), shape((hidden, n_patch)), shape((1, hidden))],
        [block, got],
        name="last",
    )
    return (
        jnp.swapaxes(final, 1, 2),
        dw_in,
        dw_out,
        db[0],
        norm[0, 0:width],
        norm[0, width : 2 * width],
    )


def role_digit(radix):
    index = lax.axis_index("dp")
    return jnp.where(lax.rem(index, 2) == 0, lax.rem(index // 2, radix), lax.axis_index("chan"))


def role_pairs(n_dp, n_chan, j, swap):
    pairs = []
    for d in range(n_dp):
        for c in range(n_chan):
            e, f = (d ^ (2 * j), c) if (d % 2 == 0) != swap else (d, c ^ j)
            pairs.append((d * n_chan + c, e * n_chan + f))
    return pairs


def role_exchange(values, n_dp, n_chan, swap=False):
    return [
        lax.ppermute(v, ("dp", "chan"), role_pairs(n_dp, n_chan, j, swap))
        for j, v in enumerate(values, 1)
    ]


def role_send_body(cot_ref, act_ref, n_ref, gp_ref, o_ref):
    core = lax.rem(lax.axis_index("dp"), 2)

    def store(v):
        o_ref[...] = v.astype(BF16)

    weight_dots(1 - core, cot_ref, act_ref, n_ref, gp_ref, store)


def role_scatter_body(radix, own_ref, got_ref, keep_ref, *sends):
    chunk = own_ref.shape[0] // radix
    me = role_digit(radix)
    for i in range(radix):
        span = slice(i * chunk, (i + 1) * chunk)
        part = own_ref[span, :] + got_ref[span, :].astype(F32)

        @pl.when(me == i)
        def _():
            keep_ref[...] = part

        for j, send in enumerate(sends, 1):

            @pl.when(me == i ^ j)
            def _():
                send[...] = part.astype(BF16)


def role_mid_body(sums_ref, norm_ref, db_ref, o_ref):
    n, patches = sums_ref.shape
    o_ref[...] = jnp.zeros_like(o_ref)
    o_ref[0:n, 0:patches] = sums_ref[...]
    o_ref[n : n + 1, :] = norm_ref[...]
    o_ref[n + 1 : n + 2, :] = db_ref[...]


def role_pack_body(n, patches, own_ref, mid_ref, mid_got_ref, *refs):
    got, (o_ref, norm_ref) = refs[:-2], refs[-2:]
    rows, hidden = own_ref.shape
    total = own_ref[...]
    for g in got:
        total = total + g[...].astype(F32)
    o_ref[0:rows, :] = total.astype(BF16)
    side = hidden - 2 * patches
    fold = hidden // side
    db = mid_ref[n + 1 : n + 2, :] + mid_got_ref[n + 1 : n + 2, :]
    folded = [v[:, k * side : (k + 1) * side] for v in high_low(db) for k in range(fold)]
    folded.append(jnp.zeros((n - 2 * fold, side), BF16))
    for k, ref in enumerate((mid_ref, mid_got_ref)):
        span = slice(rows + k * n, rows + (k + 1) * n)
        high, low = high_low(ref[0:n, 0:patches])
        o_ref[span, 0:patches] = high
        o_ref[span, patches : 2 * patches] = low
        if k == 0:
            o_ref[span, 2 * patches :] = jnp.concatenate(folded, axis=0)
        else:
            o_ref[span, 2 * patches :] = jnp.zeros((n, side), BF16)
    norm_ref[...] = mid_ref[n : n + 1, :] + mid_got_ref[n : n + 1, :]


def role_total_body(n, patches, scale, channels, norm_ref, *refs):
    every, (o_ref, mine_ref, other_ref) = refs[:-3], refs[-3:]
    rows = every[0].shape[0] - 2 * n
    hidden = every[0].shape[1]
    side = hidden - 2 * patches
    fold = hidden // side
    o_ref[0:rows, :] = (tree([r[0:rows, :].astype(F32) for r in every]) * scale).astype(BF16)
    for k, out in enumerate((mine_ref, other_ref)):
        span = slice(rows + k * n, rows + (k + 1) * n)
        pairs = [
            r[span, 0:patches].astype(F32) + r[span, patches : 2 * patches].astype(F32)
            for r in every
        ]
        out[...] = tree(pairs) / channels
    span = slice(rows, rows + n)
    folded = [r[span, 2 * patches :].astype(F32) for r in every]
    folded = tree([f[0:fold] + f[fold : 2 * fold] for f in folded])
    db = jnp.concatenate([folded[k : k + 1, :] for k in range(fold)], axis=1)
    small = [*high_low(norm_ref[...]), *high_low(db)]
    o_ref[rows:, :] = jnp.concatenate([*small, jnp.zeros((EXTRA - 4, hidden), BF16)], axis=0)


def role_input_body(
    x_ref, cot_ref, gn_ref, mr_ref, gain_ref, mine_ref, got_ref, o_ref, tick_ref, terms_ref
):
    core = lax.rem(lax.axis_index("dp"), 2)

    @pl.when(core == 0)
    def _():
        terms_ref[...] = mine_ref[...]

    @pl.when(core != 0)
    def _():
        terms_ref[...] = got_ref[...]

    input_body(x_ref, cot_ref, gn_ref, mr_ref, gain_ref, terms_ref, o_ref)
    tick_ref[...] = jnp.zeros_like(tick_ref)


def role_gather_body(radix, tick_ref, *refs):
    every, (o_ref,) = refs[:-1], refs[-1:]
    rows = every[0].shape[0] - EXTRA
    me = role_digit(radix)
    for j, r in enumerate(every):
        for i in range(radix):

            @pl.when(me == i ^ j)
            def _():
                o_ref[i * rows : (i + 1) * rows, :] = r[0:rows, :]

    small = []
    for k in (0, 2):
        total = tree(
            [r[rows + k : rows + k + 1, :].astype(F32) + r[rows + k + 1 : rows + k + 2, :].astype(F32) for r in every]
        )
        small.extend(high_low(total))
    zeros = jnp.zeros((EXTRA - 4, o_ref.shape[1]), BF16)
    o_ref[radix * rows :, :] = jnp.concatenate([*small, zeros], axis=0)


def role_last_body(scale, mine_ref, got_ref, out_ref, in_ref, db_ref, gain_ref, shift_ref):
    rows = mine_ref.shape[0] - EXTRA
    width = gain_ref.shape[0]
    core = lax.rem(lax.axis_index("dp"), 2)

    def finish(a_ref, b_ref):
        out_ref[...] = a_ref[0:rows, :].astype(F32)
        in_ref[...] = jnp.transpose(b_ref[0:rows, :].astype(F32), (1, 0))
        small = a_ref[rows : rows + 4, :].astype(F32)
        norm = (small[0:1] + small[1:2]) * scale
        db = (small[2:3] + small[3:4]) * scale
        db_ref[...] = db.reshape(db_ref.shape)
        gain_ref[...] = norm[:, 0:width].reshape(gain_ref.shape)
        shift_ref[...] = norm[:, width : 2 * width].reshape(shift_ref.shape)

    @pl.when(core == 0)
    def _():
        finish(mine_ref, got_ref)

    @pl.when(core != 0)
    def _():
        finish(got_ref, mine_ref)


def role_plan(x, cot, mr, normed, act, gp, db, gain, w_token_in, scale, channels):
    n_dp, n_chan = lax.axis_size("dp"), lax.axis_size("chan")
    images, width, n_patch = x.shape
    hidden = act.shape[2]
    n = 2 * images
    work = 2 * images * width * n_patch * hidden
    rows = n_patch // n_chan
    quad = [cot, act, normed, gp]
    pair = lambda v: exchange(v, "dp", n_dp, 1, 2)[0]

    (send,) = call(role_send_body, [shape((n_patch, hidden), BF16)], quad, work, "send")
    got = pair(send)
    (own,) = call(keep_body, [shape((n_patch, hidden))], quad, work, "keep")
    own, *sends = call(
        functools.partial(role_scatter_body, n_chan),
        [shape((rows, hidden))] + [shape((rows, hidden), BF16)] * (n_chan - 1),
        [own, got],
        name="scatter",
    )
    got = role_exchange(sends, n_dp, n_chan)
    gn, sums, norm = norm_call(x, mr, gain, gp, w_token_in, work)
    (mid,) = call(role_mid_body, [shape((n + 8, hidden))], [sums, norm, db], name="mid")
    mid_got = pair(mid)
    message, norm = call(
        functools.partial(role_pack_body, n, n_patch),
        [shape((rows + 2 * n, hidden), BF16), shape((1, hidden))],
        [own, mid, mid_got, *got],
        name="pack",
    )
    got = role_exchange([message] * (n_chan - 1), n_dp, n_chan, swap=True)
    block, mine, other = call(
        functools.partial(role_total_body, n, n_patch, scale, channels),
        [shape((rows + EXTRA, hidden), BF16), shape((n, n_patch)), shape((n, n_patch))],
        [norm, message, *got],
        name="total",
    )
    terms = pair(other)
    got = role_exchange([block] * (n_chan - 1), n_dp, n_chan)
    args = [x, cot, gn, mr, gain, mine, terms]
    final, tick = pl.pallas_call(
        role_input_body,
        out_shape=[shape(x.shape, BF16), shape((8, 128))],
        in_specs=[VM] * len(args),
        out_specs=[VM] * 2,
        scratch_shapes=[pltpu.VMEM((n, n_patch), F32)],
        name="input",
        compiler_params=LIMIT,
        cost_estimate=pl.CostEstimate(flops=work, bytes_accessed=1 << 22, transcendentals=0),
    )(*args)
    (block,) = call(
        functools.partial(role_gather_body, n_chan),
        [shape((n_patch + EXTRA, hidden), BF16)],
        [tick, block, *got],
        name="gather",
    )
    outs = [shape((n_patch, hidden)), shape((hidden, n_patch)), shape((hidden,)), shape((width,)), shape((width,))]
    dw_out, dw_in, db, d_gain, d_shift = call(
        functools.partial(role_last_body, scale), outs, [block, pair(block)], name="last"
    )
    return jnp.swapaxes(final, 1, 2), dw_in, dw_out, db, d_gain, d_shift


def shards(
    patches, cotangent, w_token_in, b_token_in, w_token_out, layer_norm_gain, layer_norm_bias
):
    n_dp, n_chan = lax.axis_size("dp"), lax.axis_size("chan")
    channels = layer_norm_gain.shape[0]
    x, cot = jnp.swapaxes(patches, 1, 2), jnp.swapaxes(cotangent, 1, 2)
    images, width, n_patch = x.shape
    hidden = w_token_in.shape[0]
    scale = 1.0 / (images * n_dp)
    work = 2 * images * width * n_patch * hidden
    assert 2 * width <= hidden and 2 * n_patch <= hidden

    (sums,) = call(stats_body, [shape((2 * images, n_patch))], [x], name="stats")
    others = exchange(sums, "chan", n_chan, 1, n_chan)
    ga, gain, bias = call(
        functools.partial(early_body, n_chan),
        [shape((images, width, hidden)), shape((width, n_patch)), shape((width, n_patch))],
        [cot, w_token_out, layer_norm_gain[None], layer_norm_bias[None]],
        flops=work,
        name="early",
    )
    args = [x, sums, *others, gain, bias, w_token_in, b_token_in[None], ga]
    outs = [
        shape((2, images, n_patch)),
        shape(x.shape, BF16),
        shape((images, width, hidden), BF16),
        shape((images, width, hidden), BF16),
        shape((1, hidden)),
    ]
    mr, normed, act, gp, db = pl.pallas_call(
        functools.partial(main_body, n_chan, channels),
        out_shape=outs,
        in_specs=[VM] * len(args),
        out_specs=[VM] * len(outs),
        scratch_shapes=[pltpu.VMEM((width, hidden), F32), pltpu.VMEM((8, hidden), F32)],
        name="main",
        compiler_params=LIMIT,
    )(*args)

    plan = role_plan if n_dp // 2 == n_chan else plain_plan
    return plan(x, cot, mr, normed, act, gp, db, gain, w_token_in, scale, channels)


def solution(mesh):
    placed = (P("dp", None, "chan"), P("dp", None, "chan"), P(), P(), P(), P(), P())
    return jax.shard_map(
        shards,
        mesh=mesh,
        in_specs=placed,
        out_specs=(P("dp", None, "chan"), P(), P(), P(), P("chan"), P("chan")),
        check_vma=False,
    )
```

```python
import functools
import math

import jax
import jax.numpy as jnp
from jax import lax
from jax.experimental import pallas as pl
from jax.experimental.pallas import tpu as pltpu
from jax.sharding import PartitionSpec as P


eps_norm = 1e-05
STEP = 32
SPREAD = 4 << 30
EXTRA = 16
F32 = jnp.float32
BF16 = jnp.bfloat16
VM = pl.BlockSpec(memory_space=pltpu.VMEM)
LIMIT = pltpu.CompilerParams(vmem_limit_bytes=24 << 20)


def call(body, outs, args, flops=0):
    nbytes = sum(a.size * a.dtype.itemsize for a in (*args, *outs))
    return pl.pallas_call(
        body,
        out_shape=outs,
        in_specs=[VM] * len(args),
        out_specs=[VM] * len(outs),
        compiler_params=LIMIT,
        cost_estimate=pl.CostEstimate(
            flops=flops, bytes_accessed=nbytes, transcendentals=0
        ),
    )(*args)


def shape(dims, dtype=F32):
    return jax.ShapeDtypeStruct(tuple(dims), dtype)


def dot(a, b, ca, cb, precision=None):
    return lax.dot_general(
        a, b, (((ca,), (cb,)), ((), ())), precision=precision, preferred_element_type=F32
    )


def high_low(v):
    high = v.astype(BF16)
    return high, (v - high.astype(F32)).astype(BF16)


def tree(values):
    values = list(values)
    while len(values) > 1:
        values = [a + b for a, b in zip(values[::2], values[1::2], strict=True)]
    return values[0]


def radices_of(n):
    factors, left = [2], n // 2
    while left > 1:
        r = 4 if left % 4 == 0 else 2
        factors.append(r)
        left //= r
    assert math.prod(factors) == n
    return factors


def exchange(value, axis, n, stride, radix):
    got = []
    for j in range(1, radix):
        got.append(lax.ppermute(value, axis, [(i, i ^ (j * stride)) for i in range(n)]))
    return got


def exchange_each(values, axis, n, stride):
    return [
        lax.ppermute(v, axis, [(i, i ^ (j * stride)) for i in range(n)])
        for j, v in enumerate(values, 1)
    ]


def tiny_rows(row, extra=EXTRA):
    high, low = high_low(row)
    return jnp.concatenate([high, low, jnp.zeros((extra - 2, row.shape[1]), BF16)], axis=0)


def join_pair(block):
    return block[0:1].astype(F32) + block[1:2].astype(F32)


def stats_body(x_ref, o_ref):
    images = x_ref.shape[0]
    for b in range(images):
        x = x_ref[b].astype(F32)
        o_ref[b : b + 1, :] = jnp.sum(x, axis=0, keepdims=True)
        o_ref[images + b : images + b + 1, :] = jnp.sum(x * x, axis=0, keepdims=True)


def spread_body(n_chan, patches, gain_ref, bias_ref, gain_o, bias_o):
    width = gain_o.shape[0]
    where = lax.axis_index("chan")
    for i in range(n_chan):

        @pl.when(where == i)
        def _():
            for src, dst in ((gain_ref, gain_o), (bias_ref, bias_o)):
                row = src[0:1, i * width : (i + 1) * width]
                rows = jnp.broadcast_to(row, (patches, width))
                dst[...] = jnp.transpose(rows, (1, 0))


def main_body(n_parts, channels, x_ref, *refs):
    parts = refs[:n_parts]
    gain_ref, bias_ref, w_ref, b_ref, cot_ref, w_out_ref = refs[n_parts : n_parts + 6]
    mr_ref, n_ref, act_ref, gp_ref, gn_ref, db_ref, *work_refs, acc_ref = refs[n_parts + 6 :]
    pre_refs, ga_refs = work_refs[:2], work_refs[2:]
    images, width, _ = x_ref.shape
    totals = tree([p[...] for p in parts]) / channels
    mean = totals[:images]
    rstd = lax.rsqrt(totals[images:] - mean * mean + eps_norm)
    mr_ref[0] = mean
    mr_ref[1] = rstd
    acc_ref[...] = jnp.zeros_like(acc_ref)
    step = STEP

    def project(b):
        xhat = (x_ref[b].astype(F32) - mr_ref[0, b : b + 1, :]) * mr_ref[1, b : b + 1, :]
        normed = (xhat * gain_ref[...] + bias_ref[...]).astype(BF16)
        n_ref[b] = normed
        pre_refs[b % 2][...] = dot(normed, w_ref[...], 1, 1)
        ga_refs[b % 2][...] = dot(cot_ref[b], w_out_ref[...], 1, 0)

    def back(b):
        gn_ref[b] = (0.5 * dot(gp_ref[b], w_ref[...], 1, 0)).astype(BF16)

    def gelu(b):
        for r in range(0, width, step):
            rows = slice(r, r + step)
            pre = pre_refs[b % 2][rows, :] + b_ref[...]
            twice = 1.0 + lax.erf(pre * (1.0 / math.sqrt(2.0)))
            act_ref[b, rows, :] = (pre * twice).astype(BF16)
            bell = jnp.exp2((pre * pre) * (-0.5 / math.log(2.0)))
            slope = twice + (pre * math.sqrt(2.0 / math.pi)) * bell
            gp = (ga_refs[b % 2][rows, :] * slope).astype(BF16)
            gp_ref[b, rows, :] = gp
            gpf = gp.astype(F32)
            acc_ref[...] += functools.reduce(
                jnp.add, [gpf[i : i + 8] for i in range(0, step, 8)]
            )

    project(0)
    for b in range(images):
        if b + 1 < images:
            project(b + 1)
        if b > 0:
            back(b - 1)
        gelu(b)
    back(images - 1)
    db_ref[...] = jnp.sum(acc_ref[...], axis=0, keepdims=True)


def weight_dots(which, cot_ref, act_ref, n_ref, gp_ref, store):
    rows = cot_ref.shape[0] * cot_ref.shape[1]

    @pl.when(which == 0)
    def _():
        store(dot(flat(cot_ref, rows), flat(act_ref, rows), 0, 0))

    @pl.when(which != 0)
    def _():
        store(dot(flat(n_ref, rows), flat(gp_ref, rows), 0, 0))


def flat(ref, rows):
    return ref[...].reshape(rows, ref.shape[2])


def send_body(cot_ref, act_ref, n_ref, gp_ref, db_ref, o_ref):
    patches = cot_ref.shape[2]
    core = lax.rem(lax.axis_index("dp"), 2)

    def store(v):
        o_ref[0:patches, :] = v.astype(BF16)

    weight_dots(1 - core, cot_ref, act_ref, n_ref, gp_ref, store)
    o_ref[patches:, :] = tiny_rows(db_ref[...])


def keep_body(cot_ref, act_ref, n_ref, gp_ref, o_ref):
    core = lax.rem(lax.axis_index("dp"), 2)

    def store(v):
        o_ref[...] = v

    weight_dots(core, cot_ref, act_ref, n_ref, gp_ref, store)


def scatter_body(radix, stride, n_got, own_ref, db_ref, *refs):
    got, (keep_ref, dbo_ref, *sends) = refs[:n_got], refs[n_got:]
    rows = own_ref.shape[0]
    chunk = rows // radix
    me = lax.rem(lax.axis_index("dp") // stride, radix)
    db = tree([join_pair(tiny_rows(db_ref[...]))] + [join_pair(g[rows:, :]) for g in got])
    dbo_ref[...] = db
    tiny = tiny_rows(db)
    for i in range(radix):
        span = slice(i * chunk, (i + 1) * chunk)
        part = own_ref[span, :]
        for g in got:
            part = part + g[span, :].astype(F32)

        @pl.when(me == i)
        def _():
            keep_ref[...] = part

        for j, send in enumerate(sends, 1):

            @pl.when(me == i ^ j)
            def _():
                send[0:chunk, :] = part.astype(BF16)

    for send in sends:
        send[chunk:, :] = tiny


def norm_body(x_ref, mr_ref, gain_ref, gn_ref, sums_ref, norm_ref, acc_ref):
    images, width, patches = x_ref.shape
    acc_ref[...] = jnp.zeros_like(acc_ref)

    def image(b, carry):
        gnf = gn_ref[b].astype(F32)
        xhat = (x_ref[b].astype(F32) - mr_ref[0, pl.ds(b, 1), :]) * mr_ref[1, pl.ds(b, 1), :]
        prod = gnf * xhat
        acc_ref[0] += prod
        acc_ref[1] += gnf
        gain = gain_ref[...]
        sums_ref[pl.ds(b, 1), :] = jnp.sum(gnf * gain, axis=0, keepdims=True)
        sums_ref[pl.ds(images + b, 1), :] = jnp.sum(prod * gain, axis=0, keepdims=True)
        return carry

    lax.fori_loop(0, images, image, 0)
    ones = jnp.ones((8, patches), F32)
    norm_ref[...] = jnp.zeros_like(norm_ref)
    for i in range(2):
        row = dot(ones, acc_ref[i], 1, 1, precision=lax.Precision.HIGHEST)
        norm_ref[0:1, i * width : (i + 1) * width] = row[0:1]


def pack_body(n_got, own_ref, db_ref, sums_ref, *refs):
    got, (o_ref,) = refs[:n_got], refs[n_got:]
    rows, hidden = own_ref.shape
    total = own_ref[...]
    for g in got:
        total = total + g[0:rows, :].astype(F32)
    o_ref[0:rows, :] = total.astype(BF16)
    db = tree([join_pair(tiny_rows(db_ref[...]))] + [join_pair(g[rows:, :]) for g in got])
    o_ref[rows : rows + EXTRA, :] = tiny_rows(db)
    n, patches = sums_ref.shape
    high, low = high_low(sums_ref[...])
    o_ref[rows + EXTRA :, :] = jnp.zeros((n, hidden), BF16)
    o_ref[rows + EXTRA :, 0:patches] = high
    o_ref[rows + EXTRA :, patches : 2 * patches] = low


def total_body(n_got, scale, channels, mine_ref, norm_ref, *refs):
    got, (o_ref, db_ref, terms_ref) = refs[:n_got], refs[n_got:]
    n, patches = terms_ref.shape
    rows = mine_ref.shape[0] - EXTRA - n
    every = (mine_ref, *got)
    o_ref[0:rows, :] = (tree([r[0:rows, :].astype(F32) for r in every]) * scale).astype(BF16)
    o_ref[rows:, :] = tiny_rows(norm_ref[...])
    db_ref[...] = tree([join_pair(r[rows : rows + EXTRA, :]) for r in every]) * scale
    sums = tree(
        [
            r[rows + EXTRA :, 0:patches].astype(F32)
            + r[rows + EXTRA :, patches : 2 * patches].astype(F32)
            for r in every
        ]
    )
    terms_ref[...] = sums / channels


def input_body(x_ref, cot_ref, gn_ref, mr_ref, gain_ref, terms_ref, o_ref):
    images = x_ref.shape[0]

    def image(b, carry):
        one = pl.ds(b, 1)
        mean, rstd = mr_ref[0, one, :], mr_ref[1, one, :]
        xhat = (x_ref[b].astype(F32) - mean) * rstd
        hat = gn_ref[b].astype(F32) * gain_ref[...]
        inner = hat - terms_ref[one, :] - xhat * terms_ref[pl.ds(images + b, 1), :]
        o_ref[b] = (cot_ref[b].astype(F32) + rstd * inner).astype(BF16)
        return carry

    lax.fori_loop(0, images, image, 0)


def gather_body(radix, stride, mine_ref, *refs):
    got, (o_ref,) = refs[:-1], refs[-1:]
    rows = mine_ref.shape[0] - EXTRA
    me = lax.rem(lax.axis_index("dp") // stride, radix)
    every = (mine_ref, *got)
    for j, r in enumerate(every):
        for i in range(radix):

            @pl.when(me == i ^ j)
            def _():
                o_ref[i * rows : (i + 1) * rows, :] = r[0:rows, :]

    o_ref[radix * rows :, :] = tiny_rows(tree([join_pair(r[rows:, :]) for r in every]))


def last_body(scale, mine_ref, got_ref, out_ref, in_ref, norm_ref):
    rows = mine_ref.shape[0] - EXTRA
    core = lax.rem(lax.axis_index("dp"), 2)
    norm_ref[...] = (join_pair(mine_ref[rows:, :]) + join_pair(got_ref[rows:, :])) * scale

    def finish(a_ref, b_ref):
        out_ref[...] = a_ref[0:rows, :].astype(F32)
        in_ref[...] = jnp.transpose(b_ref[0:rows, :].astype(F32), (1, 0))

    @pl.when(core == 0)
    def _():
        finish(mine_ref, got_ref)

    @pl.when(core != 0)
    def _():
        finish(got_ref, mine_ref)


def norm_call(x, mr, gain, gn, hidden):
    images, width, n_patch = x.shape
    return pl.pallas_call(
        norm_body,
        out_shape=[shape((2 * images, n_patch)), shape((1, hidden))],
        in_specs=[VM] * 4,
        out_specs=[VM] * 2,
        scratch_shapes=[pltpu.VMEM((2, width, n_patch), F32)],
        name="norm",
        compiler_params=LIMIT,
        cost_estimate=pl.CostEstimate(flops=1 << 29, bytes_accessed=1 << 22, transcendentals=0),
    )(x, mr, gain, gn)


def plain_plan(x, cot, mr, normed, act, gp, gn, db, gain, scale, channels):
    n_dp, n_chan = lax.axis_size("dp"), lax.axis_size("chan")
    images, width, n_patch = x.shape
    hidden = act.shape[2]
    work = 2 * images * width * n_patch * hidden
    quad = [cot, act, normed, gp]
    (send,) = call(send_body, [shape((n_patch + EXTRA, hidden), BF16)], [*quad, db], flops=work)
    radices = radices_of(n_dp)
    got = exchange_each([send], "dp", n_dp, 1)
    (own,) = call(keep_body, [shape((n_patch, hidden))], quad, flops=work)
    stride = radices[0]
    rows = n_patch
    for radix in radices[1:]:
        rows //= radix
        own, db, *sends = call(
            functools.partial(scatter_body, radix, stride, len(got)),
            [shape((rows, hidden)), shape((1, hidden))]
            + [shape((rows + EXTRA, hidden), BF16)] * (radix - 1),
            [own, db, *got],
        )
        got = exchange_each(sends, "dp", n_dp, stride)
        stride *= radix

    sums, norm = norm_call(x, mr, gain, gn, hidden)
    (message,) = call(
        functools.partial(pack_body, len(got)),
        [shape((rows + EXTRA + 2 * images, hidden), BF16)],
        [own, db, sums, *got],
    )
    others = exchange(message, "chan", n_chan, 1, n_chan)
    block, db, terms = call(
        functools.partial(total_body, len(others), 0.5 * scale, channels),
        [shape((rows + EXTRA, hidden), BF16), shape((1, hidden)), shape((2 * images, n_patch))],
        [message, norm, *others],
    )
    final = None
    for radix in radices[:0:-1]:
        stride //= radix
        got = exchange(block, "dp", n_dp, stride, radix)
        if final is None:
            (final,) = call(input_body, [shape(x.shape, BF16)], [x, cot, gn, mr, gain, terms])
        rows *= radix
        (block,) = call(
            functools.partial(gather_body, radix, stride),
            [shape((rows + EXTRA, hidden), BF16)],
            [block, *got],
        )
    (got,) = exchange(block, "dp", n_dp, 1, 2)
    dw_out, dw_in, norm = call(
        functools.partial(last_body, scale),
        [shape((n_patch, hidden)), shape((hidden, n_patch)), shape((1, hidden))],
        [block, got],
    )
    return (
        jnp.swapaxes(final, 1, 2),
        dw_in,
        dw_out,
        db[0],
        norm[0, 0:width],
        norm[0, width : 2 * width],
    )


def role_digit(radix):
    index = lax.axis_index("dp")
    return jnp.where(lax.rem(index, 2) == 0, lax.rem(index // 2, radix), lax.axis_index("chan"))


def role_pairs(n_dp, n_chan, j, swap):
    pairs = []
    for d in range(n_dp):
        for c in range(n_chan):
            e, f = (d ^ (2 * j), c) if (d % 2 == 0) != swap else (d, c ^ j)
            pairs.append((d * n_chan + c, e * n_chan + f))
    return pairs


def role_exchange(values, n_dp, n_chan, swap=False):
    got = []
    for j, v in enumerate(values, 1):
        got.append(lax.ppermute(v, ("dp", "chan"), role_pairs(n_dp, n_chan, j, swap)))
    return got


def role_send_body(cot_ref, act_ref, n_ref, gp_ref, o_ref):
    core = lax.rem(lax.axis_index("dp"), 2)

    def store(v):
        o_ref[...] = v.astype(BF16)

    weight_dots(1 - core, cot_ref, act_ref, n_ref, gp_ref, store)


def role_scatter_body(radix, own_ref, got_ref, keep_ref, *sends):
    chunk = own_ref.shape[0] // radix
    me = role_digit(radix)
    for i in range(radix):
        span = slice(i * chunk, (i + 1) * chunk)
        part = own_ref[span, :] + got_ref[span, :].astype(F32)

        @pl.when(me == i)
        def _():
            keep_ref[...] = part

        for j, send in enumerate(sends[::-1], 1):

            @pl.when(me == i ^ j)
            def _():
                send[...] = part.astype(BF16)


def role_mid_body(sums_ref, norm_ref, db_ref, o_ref):
    n, patches = sums_ref.shape
    o_ref[...] = jnp.zeros_like(o_ref)
    o_ref[0:n, 0:patches] = sums_ref[...]
    o_ref[n : n + 1, :] = norm_ref[...]
    o_ref[n + 1 : n + 2, :] = db_ref[...]


def role_pack_body(n, patches, own_ref, mid_ref, mid_got_ref, *refs):
    got, (o_ref, norm_ref) = refs[:-2], refs[-2:]
    rows, hidden = own_ref.shape
    total = own_ref[...]
    for g in got:
        total = total + g[...].astype(F32)
    o_ref[0:rows, :] = total.astype(BF16)
    side = hidden - 2 * patches
    fold = hidden // side
    db = mid_ref[n + 1 : n + 2, :] + mid_got_ref[n + 1 : n + 2, :]
    folded = [v[:, k * side : (k + 1) * side] for v in high_low(db) for k in range(fold)]
    folded.append(jnp.zeros((n - 2 * fold, side), BF16))
    o_ref[rows:, 0:patches] = mid_ref[0:n, 0:patches].astype(BF16)
    o_ref[rows:, patches : 2 * patches] = mid_got_ref[0:n, 0:patches].astype(BF16)
    o_ref[rows:, 2 * patches :] = jnp.concatenate(folded, axis=0)
    norm_ref[...] = mid_ref[n : n + 1, :] + mid_got_ref[n : n + 1, :]


def role_total_body(n, patches, scale, channels, norm_ref, *refs):
    every, (o_ref, mine_ref, other_ref) = refs[:-3], refs[-3:]
    rows = every[0].shape[0] - n
    hidden = every[0].shape[1]
    side = hidden - 2 * patches
    fold = hidden // side
    span = slice(rows, rows + n)
    o_ref[0:rows, :] = (tree([r[0:rows, :].astype(F32) for r in every]) * scale).astype(BF16)
    for k, out in enumerate((mine_ref, other_ref)):
        lanes = slice(k * patches, (k + 1) * patches)
        out[...] = tree([r[span, lanes].astype(F32) for r in every]) / channels
    folded = [r[span, 2 * patches :].astype(F32) for r in every]
    folded = tree([f[0:fold] + f[fold : 2 * fold] for f in folded])
    db = jnp.concatenate([folded[k : k + 1, :] for k in range(fold)], axis=1)
    small = [*high_low(norm_ref[...]), *high_low(db)]
    o_ref[rows:, :] = jnp.concatenate([*small, jnp.zeros((EXTRA - 4, hidden), BF16)], axis=0)


def role_input_body(
    x_ref, cot_ref, gn_ref, mr_ref, gain_ref, mine_ref, got_ref, o_ref, tick_ref, terms_ref
):
    core = lax.rem(lax.axis_index("dp"), 2)

    @pl.when(core == 0)
    def _():
        terms_ref[...] = mine_ref[...]

    @pl.when(core != 0)
    def _():
        terms_ref[...] = got_ref[...]

    input_body(x_ref, cot_ref, gn_ref, mr_ref, gain_ref, terms_ref, o_ref)
    tick_ref[...] = jnp.zeros_like(tick_ref)


def role_gather_body(radix, tick_ref, *refs):
    every, (o_ref,) = refs[:-1], refs[-1:]
    rows = every[0].shape[0] - EXTRA
    me = role_digit(radix)
    for j, r in enumerate(every):
        for i in range(radix):

            @pl.when(me == i ^ j)
            def _():
                o_ref[i * rows : (i + 1) * rows, :] = r[0:rows, :]

    small = []
    for k in (0, 2):
        total = tree(
            [r[rows + k : rows + k + 1, :].astype(F32) + r[rows + k + 1 : rows + k + 2, :].astype(F32) for r in every]
        )
        small.extend(high_low(total))
    zeros = jnp.zeros((EXTRA - 4, o_ref.shape[1]), BF16)
    o_ref[radix * rows :, :] = jnp.concatenate([*small, zeros], axis=0)


def role_last_body(scale, mine_ref, got_ref, out_ref, in_ref, db_ref, gain_ref, shift_ref):
    rows = mine_ref.shape[0] - EXTRA
    width = gain_ref.shape[0]
    core = lax.rem(lax.axis_index("dp"), 2)

    def finish(a_ref, b_ref):
        out_ref[...] = a_ref[0:rows, :].astype(F32)
        in_ref[...] = jnp.transpose(b_ref[0:rows, :].astype(F32), (1, 0))
        small = a_ref[rows : rows + 4, :].astype(F32)
        norm = (small[0:1] + small[1:2]) * scale
        db = (small[2:3] + small[3:4]) * (0.5 * scale)
        db_ref[...] = db.reshape(db_ref.shape)
        gain_ref[...] = norm[:, 0:width].reshape(gain_ref.shape)
        shift_ref[...] = norm[:, width : 2 * width].reshape(shift_ref.shape)

    @pl.when(core == 0)
    def _():
        finish(mine_ref, got_ref)

    @pl.when(core != 0)
    def _():
        finish(got_ref, mine_ref)


def role_plan(x, cot, mr, normed, act, gp, gn, db, gain, scale, channels):
    n_dp, n_chan = lax.axis_size("dp"), lax.axis_size("chan")
    images, width, n_patch = x.shape
    hidden = act.shape[2]
    n = 2 * images
    work = 2 * images * width * n_patch * hidden
    rows = n_patch // n_chan
    quad = [cot, act, normed, gp]
    pair = lambda v: exchange(v, "dp", n_dp, 1, 2)[0]

    (send,) = call(role_send_body, [shape((n_patch, hidden), BF16)], quad, work)
    got = pair(send)
    (own,) = call(keep_body, [shape((n_patch, hidden))], quad, work)
    own, *sends = call(
        functools.partial(role_scatter_body, n_chan),
        [shape((rows, hidden))] + [shape((rows, hidden), BF16)] * (n_chan - 1),
        [own, got],
    )
    got = role_exchange(sends[::-1], n_dp, n_chan)
    sums, norm = norm_call(x, mr, gain, gn, hidden)
    (mid,) = call(role_mid_body, [shape((n + 8, hidden))], [sums, norm, db])
    mid_got = pair(mid)
    message, norm = call(
        functools.partial(role_pack_body, n, n_patch),
        [shape((rows + n, hidden), BF16), shape((1, hidden))],
        [own, mid, mid_got, *got],
    )
    got = role_exchange([message] * (n_chan - 1), n_dp, n_chan, swap=True)
    block, mine, other = call(
        functools.partial(role_total_body, n, n_patch, 0.5 * scale, channels),
        [shape((rows + EXTRA, hidden), BF16), shape((n, n_patch)), shape((n, n_patch))],
        [norm, message, *got],
    )
    terms = pair(other)
    got = role_exchange([block] * (n_chan - 1), n_dp, n_chan)
    args = [x, cot, gn, mr, gain, mine, terms]
    final, tick = pl.pallas_call(
        role_input_body,
        out_shape=[shape(x.shape, BF16), shape((8, 128))],
        in_specs=[VM] * len(args),
        out_specs=[VM] * 2,
        scratch_shapes=[pltpu.VMEM((n, n_patch), F32)],
        name="input",
        compiler_params=LIMIT,
        cost_estimate=pl.CostEstimate(flops=work, bytes_accessed=1 << 22, transcendentals=0),
    )(*args)
    (block,) = call(
        functools.partial(role_gather_body, n_chan),
        [shape((n_patch + EXTRA, hidden), BF16)],
        [tick, block, *got],
    )
    outs = [shape((n_patch, hidden)), shape((hidden, n_patch)), shape((hidden,)), shape((width,)), shape((width,))]
    dw_out, dw_in, db, d_gain, d_shift = call(
        functools.partial(role_last_body, scale), outs, [block, pair(block)]
    )
    return jnp.swapaxes(final, 1, 2), dw_in, dw_out, db, d_gain, d_shift


def shards(
    patches, cotangent, w_token_in, b_token_in, w_token_out, layer_norm_gain, layer_norm_bias
):
    n_dp, n_chan = lax.axis_size("dp"), lax.axis_size("chan")
    channels = layer_norm_gain.shape[0]
    x, cot = jnp.swapaxes(patches, 1, 2), jnp.swapaxes(cotangent, 1, 2)
    images, width, n_patch = x.shape
    hidden = w_token_in.shape[0]
    scale = 1.0 / (images * n_dp)
    assert 2 * width <= hidden and 2 * n_patch <= hidden

    (sums,) = call(stats_body, [shape((2 * images, n_patch))], [x])
    others = exchange(sums, "chan", n_chan, 1, n_chan)
    gain, bias = call(
        functools.partial(spread_body, n_chan, n_patch),
        [shape((width, n_patch)), shape((width, n_patch))],
        [layer_norm_gain[None], layer_norm_bias[None]],
        flops=SPREAD,
    )
    args = [x, sums, *others, gain, bias, w_token_in, b_token_in[None], cot, w_token_out]
    outs = [
        shape((2, images, n_patch)),
        shape(x.shape, BF16),
        shape((images, width, hidden), BF16),
        shape((images, width, hidden), BF16),
        shape(x.shape, BF16),
        shape((1, hidden)),
    ]
    mr, normed, act, gp, gn, db = pl.pallas_call(
        functools.partial(main_body, n_chan, channels),
        out_shape=outs,
        in_specs=[VM] * len(args),
        out_specs=[VM] * len(outs),
        scratch_shapes=[pltpu.VMEM((width, hidden), F32)] * 4 + [pltpu.VMEM((8, hidden), F32)],
        name="main",
        compiler_params=LIMIT,
    )(*args)

    plan = role_plan if n_dp // 2 == n_chan else plain_plan
    return plan(x, cot, mr, normed, act, gp, gn, db, gain, scale, channels)


def solution(mesh):
    placed = (P("dp", None, "chan"), P("dp", None, "chan"), P(), P(), P(), P(), P())

    return jax.shard_map(
        shards,
        mesh=mesh,
        in_specs=placed,
        out_specs=(P("dp", None, "chan"), P(), P(), P(), P("chan"), P("chan")),
        check_vma=False,
    )
```

```python
import functools
import math

import jax
import jax.numpy as jnp
from jax import lax
from jax.experimental import pallas as pl
from jax.experimental.pallas import tpu as pltpu
from jax.sharding import PartitionSpec as P


eps_norm = 1e-05
STEP = 32
SPREAD = 4 << 30
EXTRA = 16
F32 = jnp.float32
BF16 = jnp.bfloat16
VM = pl.BlockSpec(memory_space=pltpu.VMEM)
HB = pl.BlockSpec(memory_space=pltpu.HBM)
LIMIT = pltpu.CompilerParams(vmem_limit_bytes=24 << 20)


def call(body, outs, args, flops=0):
    nbytes = sum(a.size * a.dtype.itemsize for a in (*args, *outs))
    return pl.pallas_call(
        body,
        out_shape=outs,
        in_specs=[VM] * len(args),
        out_specs=[VM] * len(outs),
        compiler_params=LIMIT,
        cost_estimate=pl.CostEstimate(
            flops=flops, bytes_accessed=nbytes, transcendentals=0
        ),
    )(*args)


def shape(dims, dtype=F32):
    return jax.ShapeDtypeStruct(tuple(dims), dtype)


def dot(a, b, ca, cb, precision=None):
    return lax.dot_general(
        a, b, (((ca,), (cb,)), ((), ())), precision=precision, preferred_element_type=F32
    )


def high_low(v):
    high = v.astype(BF16)
    return high, (v - high.astype(F32)).astype(BF16)


def tree(values):
    values = list(values)
    while len(values) > 1:
        values = [a + b for a, b in zip(values[::2], values[1::2], strict=True)]
    return values[0]


def radices_of(n):
    factors, left = [2], n // 2
    while left > 1:
        r = 4 if left % 4 == 0 else 2
        factors.append(r)
        left //= r
    assert math.prod(factors) == n
    return factors


def exchange(value, axis, n, stride, radix):
    got = []
    for j in range(1, radix):
        got.append(lax.ppermute(value, axis, [(i, i ^ (j * stride)) for i in range(n)]))
    return got


def exchange_each(values, axis, n, stride):
    return [
        lax.ppermute(v, axis, [(i, i ^ (j * stride)) for i in range(n)])
        for j, v in enumerate(values, 1)
    ]


def tiny_rows(row, extra=EXTRA):
    high, low = high_low(row)
    return jnp.concatenate([high, low, jnp.zeros((extra - 2, row.shape[1]), BF16)], axis=0)


def join_pair(block):
    return block[0:1].astype(F32) + block[1:2].astype(F32)


def stats_body(x_ref, o_ref):
    images = x_ref.shape[0]
    for b in range(images):
        x = x_ref[b].astype(F32)
        o_ref[b : b + 1, :] = jnp.sum(x, axis=0, keepdims=True)
        o_ref[images + b : images + b + 1, :] = jnp.sum(x * x, axis=0, keepdims=True)


def spread_body(n_chan, patches, gain_ref, bias_ref, gain_o, bias_o):
    width = gain_o.shape[0]
    where = lax.axis_index("chan")
    for i in range(n_chan):

        @pl.when(where == i)
        def _():
            for src, dst in ((gain_ref, gain_o), (bias_ref, bias_o)):
                row = src[0:1, i * width : (i + 1) * width]
                rows = jnp.broadcast_to(row, (patches, width))
                dst[...] = jnp.transpose(rows, (1, 0))


def main_body(n_parts, channels, x_ref, *refs):
    parts = refs[:n_parts]
    gain_ref, bias_ref, w_ref, b_ref, cot_ref, w_out_ref = refs[n_parts : n_parts + 6]
    mr_ref, n_ref, act_ref, gp_ref, send_ref, *work_refs, acc_ref = refs[n_parts + 6 :]
    pre_refs, ga_refs = work_refs[:2], work_refs[2:]
    images, width, patches = x_ref.shape
    totals = tree([p[...] for p in parts]) / channels
    mean = totals[:images]
    rstd = lax.rsqrt(totals[images:] - mean * mean + eps_norm)
    mr_ref[0] = mean
    mr_ref[1] = rstd
    core = lax.rem(lax.axis_index("dp"), 2)
    step = STEP

    def project(b):
        xhat = (x_ref[b].astype(F32) - mr_ref[0, b : b + 1, :]) * mr_ref[1, b : b + 1, :]
        normed = (xhat * gain_ref[...] + bias_ref[...]).astype(BF16)
        n_ref[b] = normed
        pre_refs[b % 2][...] = dot(normed, w_ref[...], 1, 1)
        ga_refs[b % 2][...] = dot(cot_ref[b], w_out_ref[...], 1, 0)

    def partner_grad(b):
        pair, rows = slice(b, b + 2), 2 * width
        left = jnp.where(core == 0, n_ref[pair], cot_ref[pair]).reshape(rows, patches)
        right = jnp.where(core == 0, gp_ref[pair], act_ref[pair]).reshape(rows, gp_ref.shape[2])
        part = dot(left, right, 0, 0)
        acc_ref[...] = part if b == 0 else acc_ref[...] + part

    def gelu(b):
        for r in range(0, width, step):
            rows = slice(r, r + step)
            pre = pre_refs[b % 2][rows, :] + b_ref[...]
            twice = 1.0 + lax.erf(pre * (1.0 / math.sqrt(2.0)))
            act_ref[b, rows, :] = (pre * twice).astype(BF16)
            bell = jnp.exp2((pre * pre) * (-0.5 / math.log(2.0)))
            slope = twice + (pre * math.sqrt(2.0 / math.pi)) * bell
            gp_ref[b, rows, :] = (ga_refs[b % 2][rows, :] * slope).astype(BF16)

    project(0)
    for b in range(images):
        if b + 1 < images:
            project(b + 1)
        if b > 0 and b % 2 == 0:
            partner_grad(b - 2)
        gelu(b)
    partner_grad(images - 2)
    send_ref[...] = acc_ref[...].astype(BF16)


def weight_dots(which, cot_ref, act_ref, n_ref, gp_ref, store):
    rows = cot_ref.shape[0] * cot_ref.shape[1]

    @pl.when(which == 0)
    def _():
        store(dot(flat(cot_ref, rows), flat(act_ref, rows), 0, 0))

    @pl.when(which != 0)
    def _():
        store(dot(flat(n_ref, rows), flat(gp_ref, rows), 0, 0))


def flat(ref, rows):
    return ref[...].reshape(rows, ref.shape[2])


def send_body(cot_ref, act_ref, n_ref, gp_ref, db_ref, o_ref):
    patches = cot_ref.shape[2]
    core = lax.rem(lax.axis_index("dp"), 2)

    def store(v):
        o_ref[0:patches, :] = v.astype(BF16)

    weight_dots(1 - core, cot_ref, act_ref, n_ref, gp_ref, store)
    o_ref[patches:, :] = tiny_rows(db_ref[...])


def keep_body(cot_ref, act_ref, n_ref, gp_ref, o_ref):
    core = lax.rem(lax.axis_index("dp"), 2)

    def store(v):
        o_ref[...] = v

    weight_dots(core, cot_ref, act_ref, n_ref, gp_ref, store)


def scatter_body(radix, stride, n_got, own_ref, db_ref, *refs):
    got, (keep_ref, dbo_ref, *sends) = refs[:n_got], refs[n_got:]
    rows = own_ref.shape[0]
    chunk = rows // radix
    me = lax.rem(lax.axis_index("dp") // stride, radix)
    db = tree([join_pair(tiny_rows(db_ref[...]))] + [join_pair(g[rows:, :]) for g in got])
    dbo_ref[...] = db
    tiny = tiny_rows(db)
    for i in range(radix):
        span = slice(i * chunk, (i + 1) * chunk)
        part = own_ref[span, :]
        for g in got:
            part = part + g[span, :].astype(F32)

        @pl.when(me == i)
        def _():
            keep_ref[...] = part

        for j, send in enumerate(sends, 1):

            @pl.when(me == i ^ j)
            def _():
                send[0:chunk, :] = part.astype(BF16)

    for send in sends:
        send[chunk:, :] = tiny


def back_body(x_ref, mr_ref, gain_ref, gp_ref, w_ref, gn_ref, sums_ref, db_ref, acc_ref):
    images, width = x_ref.shape[0], x_ref.shape[1]

    def project(b):
        gn_ref[b] = (0.5 * dot(gp_ref[b], w_ref[...], 1, 0)).astype(BF16)

    def reduce(b):
        xhat = (x_ref[b].astype(F32) - mr_ref[0, b : b + 1, :]) * mr_ref[1, b : b + 1, :]
        hat = gn_ref[b].astype(F32) * gain_ref[...]
        sums_ref[b : b + 1, :] = jnp.sum(hat, axis=0, keepdims=True)
        sums_ref[images + b : images + b + 1, :] = jnp.sum(hat * xhat, axis=0, keepdims=True)
        gp = gp_ref[b].astype(F32)
        part = functools.reduce(jnp.add, [gp[i : i + 8] for i in range(0, width, 8)])
        acc_ref[...] = part if b == 0 else acc_ref[...] + part

    project(0)
    for b in range(images):
        if b + 1 < images:
            project(b + 1)
        reduce(b)
    db_ref[...] = jnp.sum(acc_ref[...], axis=0, keepdims=True)


def back_call(x, mr, gain, gp, w_token_in):
    images, _, n_patch = x.shape
    hidden = gp.shape[2]
    return pl.pallas_call(
        back_body,
        out_shape=[shape(x.shape, BF16), shape((2 * images, n_patch)), shape((1, hidden))],
        in_specs=[VM] * 5,
        out_specs=[VM] * 3,
        scratch_shapes=[pltpu.VMEM((8, hidden), F32)],
        name="back",
        compiler_params=LIMIT,
        cost_estimate=pl.CostEstimate(flops=1 << 30, bytes_accessed=1 << 22, transcendentals=0),
    )(x, mr, gain, gp, w_token_in)


def norm_body(x_ref, mr_ref, gn_ref, norm_ref, acc_ref):
    images, width, patches = x_ref.shape
    acc_ref[...] = jnp.zeros_like(acc_ref)

    def image(b, carry):
        gnf = gn_ref[b].astype(F32)
        xhat = (x_ref[b].astype(F32) - mr_ref[0, pl.ds(b, 1), :]) * mr_ref[1, pl.ds(b, 1), :]
        acc_ref[0] += gnf * xhat
        acc_ref[1] += gnf
        return carry

    lax.fori_loop(0, images, image, 0)
    ones = jnp.ones((8, patches), F32)
    norm_ref[...] = jnp.zeros_like(norm_ref)
    for i in range(2):
        row = dot(ones, acc_ref[i], 1, 1, precision=lax.Precision.HIGHEST)
        norm_ref[0:1, i * width : (i + 1) * width] = row[0:1]


def pack_body(n_got, own_ref, db_ref, sums_ref, *refs):
    got, (o_ref,) = refs[:n_got], refs[n_got:]
    rows, hidden = own_ref.shape
    total = own_ref[...]
    for g in got:
        total = total + g[0:rows, :].astype(F32)
    o_ref[0:rows, :] = total.astype(BF16)
    db = tree([join_pair(tiny_rows(db_ref[...]))] + [join_pair(g[rows:, :]) for g in got])
    o_ref[rows : rows + EXTRA, :] = tiny_rows(db)
    n, patches = sums_ref.shape
    high, low = high_low(sums_ref[...])
    o_ref[rows + EXTRA :, :] = jnp.zeros((n, hidden), BF16)
    o_ref[rows + EXTRA :, 0:patches] = high
    o_ref[rows + EXTRA :, patches : 2 * patches] = low


def total_body(n_got, scale, channels, mine_ref, norm_ref, *refs):
    got, (o_ref, db_ref, terms_ref) = refs[:n_got], refs[n_got:]
    n, patches = terms_ref.shape
    rows = mine_ref.shape[0] - EXTRA - n
    every = (mine_ref, *got)
    o_ref[0:rows, :] = (tree([r[0:rows, :].astype(F32) for r in every]) * scale).astype(BF16)
    o_ref[rows:, :] = tiny_rows(norm_ref[...])
    db_ref[...] = tree([join_pair(r[rows : rows + EXTRA, :]) for r in every]) * scale
    sums = tree(
        [
            r[rows + EXTRA :, 0:patches].astype(F32)
            + r[rows + EXTRA :, patches : 2 * patches].astype(F32)
            for r in every
        ]
    )
    terms_ref[...] = sums / channels


def input_body(x_ref, cot_ref, gn_ref, mr_ref, gain_ref, terms_ref, o_ref):
    images = x_ref.shape[0]

    def image(b, carry):
        one = pl.ds(b, 1)
        mean, rstd = mr_ref[0, one, :], mr_ref[1, one, :]
        xhat = (x_ref[b].astype(F32) - mean) * rstd
        hat = gn_ref[b].astype(F32) * gain_ref[...]
        inner = hat - terms_ref[one, :] - xhat * terms_ref[pl.ds(images + b, 1), :]
        o_ref[b] = (cot_ref[b].astype(F32) + rstd * inner).astype(BF16)
        return carry

    lax.fori_loop(0, images, image, 0)


def gather_body(radix, stride, mine_ref, *refs):
    got, (o_ref,) = refs[:-1], refs[-1:]
    rows = mine_ref.shape[0] - EXTRA
    me = lax.rem(lax.axis_index("dp") // stride, radix)
    every = (mine_ref, *got)
    for j, r in enumerate(every):
        for i in range(radix):

            @pl.when(me == i ^ j)
            def _():
                o_ref[i * rows : (i + 1) * rows, :] = r[0:rows, :]

    o_ref[radix * rows :, :] = tiny_rows(tree([join_pair(r[rows:, :]) for r in every]))


def last_body(scale, mine_ref, got_ref, out_ref, in_ref, norm_ref):
    rows = mine_ref.shape[0] - EXTRA
    core = lax.rem(lax.axis_index("dp"), 2)
    norm_ref[...] = (join_pair(mine_ref[rows:, :]) + join_pair(got_ref[rows:, :])) * scale

    def finish(a_ref, b_ref):
        out_ref[...] = a_ref[0:rows, :].astype(F32)
        in_ref[...] = jnp.transpose(b_ref[0:rows, :].astype(F32), (1, 0))

    @pl.when(core == 0)
    def _():
        finish(mine_ref, got_ref)

    @pl.when(core != 0)
    def _():
        finish(got_ref, mine_ref)


def norm_call(x, mr, gn, hidden):
    _, width, n_patch = x.shape
    return pl.pallas_call(
        norm_body,
        out_shape=shape((1, hidden)),
        in_specs=[VM] * 3,
        out_specs=VM,
        scratch_shapes=[pltpu.VMEM((2, width, n_patch), F32)],
        name="norm",
        compiler_params=LIMIT,
        cost_estimate=pl.CostEstimate(flops=1 << 29, bytes_accessed=1 << 22, transcendentals=0),
    )(x, mr, gn)


def plain_plan(x, cot, mr, normed, act, gp, send, gain, w_token_in, scale, channels):
    n_dp, n_chan = lax.axis_size("dp"), lax.axis_size("chan")
    images, width, n_patch = x.shape
    hidden = act.shape[2]
    work = 2 * images * width * n_patch * hidden
    gn, sums, db = back_call(x, mr, gain, gp, w_token_in)
    quad = [cot, act, normed, gp]
    (send,) = call(send_body, [shape((n_patch + EXTRA, hidden), BF16)], [*quad, db], flops=work)
    radices = radices_of(n_dp)
    got = exchange_each([send], "dp", n_dp, 1)
    (own,) = call(keep_body, [shape((n_patch, hidden))], quad, flops=work)
    stride = radices[0]
    rows = n_patch
    for radix in radices[1:]:
        rows //= radix
        own, db, *sends = call(
            functools.partial(scatter_body, radix, stride, len(got)),
            [shape((rows, hidden)), shape((1, hidden))]
            + [shape((rows + EXTRA, hidden), BF16)] * (radix - 1),
            [own, db, *got],
        )
        got = exchange_each(sends, "dp", n_dp, stride)
        stride *= radix

    norm = norm_call(x, mr, gn, hidden)
    (message,) = call(
        functools.partial(pack_body, len(got)),
        [shape((rows + EXTRA + 2 * images, hidden), BF16)],
        [own, db, sums, *got],
    )
    others = exchange(message, "chan", n_chan, 1, n_chan)
    block, db, terms = call(
        functools.partial(total_body, len(others), 0.5 * scale, channels),
        [shape((rows + EXTRA, hidden), BF16), shape((1, hidden)), shape((2 * images, n_patch))],
        [message, norm, *others],
    )
    final = None
    for radix in radices[:0:-1]:
        stride //= radix
        got = exchange(block, "dp", n_dp, stride, radix)
        if final is None:
            (final,) = call(input_body, [shape(x.shape, BF16)], [x, cot, gn, mr, gain, terms])
        rows *= radix
        (block,) = call(
            functools.partial(gather_body, radix, stride),
            [shape((rows + EXTRA, hidden), BF16)],
            [block, *got],
        )
    (got,) = exchange(block, "dp", n_dp, 1, 2)
    dw_out, dw_in, norm = call(
        functools.partial(last_body, scale),
        [shape((n_patch, hidden)), shape((hidden, n_patch)), shape((1, hidden))],
        [block, got],
    )
    return (
        jnp.swapaxes(final, 1, 2),
        dw_in,
        dw_out,
        db[0],
        norm[0, 0:width],
        norm[0, width : 2 * width],
    )


def role_digit(radix):
    index = lax.axis_index("dp")
    return jnp.where(lax.rem(index, 2) == 0, lax.rem(index // 2, radix), lax.axis_index("chan"))


def role_pairs(n_dp, n_chan, j, swap):
    pairs = []
    for d in range(n_dp):
        for c in range(n_chan):
            e, f = (d ^ (2 * j), c) if (d % 2 == 0) != swap else (d, c ^ j)
            pairs.append((d * n_chan + c, e * n_chan + f))
    return pairs


def role_exchange(values, n_dp, n_chan, swap=False):
    got = []
    for j, v in reversed(list(enumerate(values, 1))):
        got.append(lax.ppermute(v, ("dp", "chan"), role_pairs(n_dp, n_chan, j, swap)))
    return got[::-1]


def role_scatter_body(radix, own_ref, got_ref, keep_ref, *sends):
    chunk = own_ref.shape[0] // radix
    me = role_digit(radix)
    for i in range(radix):
        span = slice(i * chunk, (i + 1) * chunk)
        part = own_ref[span, :] + got_ref[span, :].astype(F32)

        @pl.when(me == i)
        def _():
            keep_ref[...] = part

        for j, send in enumerate(sends[::-1], 1):

            @pl.when(me == i ^ j)
            def _():
                send[...] = part.astype(BF16)


def side_block(sums, db, hidden):
    images, patches = sums.shape[0] // 2, sums.shape[1]
    side = hidden - 2 * patches
    folded = [db[:, k : k + side] for k in range(0, hidden, side)]
    folded.append(jnp.zeros((images - len(folded), side), F32))
    parts = [sums[:images], sums[images:], jnp.concatenate(folded, axis=0)]
    return jnp.concatenate(parts, axis=1).astype(BF16)


def side_db(block, patches):
    side = block.shape[1] - 2 * patches
    fold = block.shape[1] // side
    return jnp.concatenate([block[k : k + 1, 2 * patches :] for k in range(fold)], axis=1)


def side_fits(images, patches, hidden):
    side = hidden - 2 * patches
    return side > 0 and side % 128 == 0 and hidden % side == 0 and max(4, hidden // side) <= images


def role_pack_body(own_ref, sums_ref, db_ref, *refs):
    got, (o_ref,) = refs[:-1], refs[-1:]
    rows, hidden = own_ref.shape
    total = own_ref[...]
    for g in got:
        total = total + g[...].astype(F32)
    o_ref[0:rows, :] = total.astype(BF16)
    o_ref[rows:, :] = side_block(sums_ref[...], db_ref[...], hidden)


def role_total_body(scale, norm_ref, norm_got_ref, sums_ref, *refs):
    every, (o_ref,) = refs[:-1], refs[-1:]
    images, patches = sums_ref.shape[0] // 2, sums_ref.shape[1]
    rows, hidden = o_ref.shape[0] - images, o_ref.shape[1]
    core = lax.rem(lax.axis_index("dp"), 2)
    o_ref[0:rows, :] = (tree([r[0:rows, :].astype(F32) for r in every]) * scale).astype(BF16)
    db = side_db(tree([r[rows:, :].astype(F32) for r in every]), patches)

    @pl.when(core == 0)
    def _():
        small = [*high_low(norm_ref[...] + norm_got_ref[...]), *high_low(db)]
        small.append(jnp.zeros((images - 4, hidden), BF16))
        o_ref[rows:, :] = jnp.concatenate(small, axis=0)

    @pl.when(core != 0)
    def _():
        o_ref[rows:, :] = side_block(sums_ref[...], db, hidden)


def role_input_body(radix, channels, x_ref, cot_ref, gn_ref, mr_ref, gain_ref, *refs):
    even, odd = refs[:radix], refs[radix : 2 * radix]
    o_hbm, terms_ref, o_ref, sems = refs[2 * radix :]
    images, patches = x_ref.shape[0], x_ref.shape[2]
    rows = even[0].shape[0] - images
    core = lax.rem(lax.axis_index("dp"), 2)

    def terms(every):
        for k in range(2):
            lanes = slice(k * patches, (k + 1) * patches)
            total = tree([r[rows:, lanes].astype(F32) for r in every])
            terms_ref[k * images : (k + 1) * images, :] = total / channels

    @pl.when(core == 0)
    def _():
        terms(even)

    @pl.when(core != 0)
    def _():
        terms(odd)

    copies = []
    for b in range(images):
        mean, rstd = mr_ref[0, b : b + 1, :], mr_ref[1, b : b + 1, :]
        xhat = (x_ref[b].astype(F32) - mean) * rstd
        hat = gn_ref[b].astype(F32) * gain_ref[...]
        inner = hat - terms_ref[b : b + 1, :] - xhat * terms_ref[images + b : images + b + 1, :]
        o_ref[b] = (cot_ref[b].astype(F32) + rstd * inner).astype(BF16)
        copy = pltpu.make_async_copy(o_ref.at[b], o_hbm.at[b], sems.at[b])
        copy.start()
        copies.append(copy)
    for copy in copies:
        copy.wait()


def role_last_body(radix, scale, *refs):
    mine, got = refs[:radix], refs[radix : 2 * radix]
    out_ref, in_ref, db_ref, gain_ref, shift_ref, held_ref = refs[2 * radix :]
    width = gain_ref.shape[0]
    patches, _ = out_ref.shape
    rows = patches // radix
    core = lax.rem(lax.axis_index("dp"), 2)
    first = lax.rem(lax.axis_index("dp") // 2, radix)
    second = lax.axis_index("chan")

    def place(dst, digit, j, ref):
        for i in range(radix):

            @pl.when(digit == i ^ j)
            def _():
                dst[i * rows : (i + 1) * rows, :] = ref[0:rows, :].astype(dst.dtype)

    def finish(outs, ins):
        for j in range(radix):
            place(out_ref, first, j, outs[j])
            place(held_ref, second, j, ins[j])
        small = tree([r[rows : rows + 4, :].astype(F32) for r in outs])
        norm = (small[0:1] + small[1:2]) * scale
        db = small[2:3] + small[3:4] + side_db(tree([r[rows:, :].astype(F32) for r in ins]), patches)
        db = db * (0.5 * scale)
        db_ref[...] = db.reshape(db_ref.shape)
        gain_ref[...] = norm[:, 0:width].reshape(gain_ref.shape)
        shift_ref[...] = norm[:, width : 2 * width].reshape(shift_ref.shape)

    @pl.when(core == 0)
    def _():
        finish(mine, got)

    @pl.when(core != 0)
    def _():
        finish(got, mine)

    in_ref[...] = jnp.transpose(held_ref[...].astype(F32), (1, 0))


def role_plan(x, cot, mr, normed, act, gp, send, gain, w_token_in, scale, channels):
    n_dp, n_chan = lax.axis_size("dp"), lax.axis_size("chan")
    images, width, n_patch = x.shape
    hidden = act.shape[2]
    work = 2 * images * width * n_patch * hidden
    rows = n_patch // n_chan
    quad = [cot, act, normed, gp]
    pair = lambda v: exchange(v, "dp", n_dp, 1, 2)[0]

    got = pair(send)
    (own,) = call(keep_body, [shape((n_patch, hidden))], quad, work)
    own, *sends = call(
        functools.partial(role_scatter_body, n_chan),
        [shape((rows, hidden))] + [shape((rows, hidden), BF16)] * (n_chan - 1),
        [own, got],
    )
    got = role_exchange(sends[::-1], n_dp, n_chan)
    gn, sums, db = back_call(x, mr, gain, gp, w_token_in)
    (message,) = call(role_pack_body, [shape((rows + images, hidden), BF16)], [own, sums, db, *got])
    got = role_exchange([message] * (n_chan - 1), n_dp, n_chan, swap=True)
    norm = norm_call(x, mr, gn, hidden)
    norm_got = pair(norm)
    messages = [message, *got]
    (block,) = call(
        functools.partial(role_total_body, 0.5 * scale),
        [shape((rows + images, hidden), BF16)],
        [norm, norm_got, sums, *messages],
    )
    got = role_exchange([block] * (n_chan - 1), n_dp, n_chan)
    every = [block, *got]
    args = [x, cot, gn, mr, gain, *messages, *every]
    final = pl.pallas_call(
        functools.partial(role_input_body, n_chan, channels),
        out_shape=shape(x.shape, BF16),
        in_specs=[VM] * len(args),
        out_specs=HB,
        scratch_shapes=[
            pltpu.VMEM((2 * images, n_patch), F32),
            pltpu.VMEM(x.shape, BF16),
            pltpu.SemaphoreType.DMA((images,)),
        ],
        name="input",
        compiler_params=LIMIT,
        cost_estimate=pl.CostEstimate(flops=work, bytes_accessed=1 << 22, transcendentals=0),
    )(*args)
    onward = {}
    for j in (0, *range(n_chan - 1, 0, -1)):
        onward[j] = pair(every[j])
    args = [*every, *(onward[j] for j in range(n_chan))]
    dw_out, dw_in, db, d_gain, d_shift = pl.pallas_call(
        functools.partial(role_last_body, n_chan, scale),
        out_shape=[
            shape((n_patch, hidden)),
            shape((hidden, n_patch)),
            shape((hidden,)),
            shape((width,)),
            shape((width,)),
        ],
        in_specs=[VM] * len(args),
        out_specs=[VM] * 5,
        scratch_shapes=[
            pltpu.VMEM((n_patch, hidden), BF16),
        ],
        name="last",
        compiler_params=LIMIT,
    )(*args)
    return jnp.swapaxes(final, 1, 2), dw_in, dw_out, db, d_gain, d_shift


def shards(
    patches, cotangent, w_token_in, b_token_in, w_token_out, layer_norm_gain, layer_norm_bias
):
    n_dp, n_chan = lax.axis_size("dp"), lax.axis_size("chan")
    channels = layer_norm_gain.shape[0]
    x, cot = jnp.swapaxes(patches, 1, 2), jnp.swapaxes(cotangent, 1, 2)
    images, width, n_patch = x.shape
    hidden = w_token_in.shape[0]
    scale = 1.0 / (images * n_dp)
    assert 2 * width <= hidden and 2 * n_patch <= hidden

    (sums,) = call(stats_body, [shape((2 * images, n_patch))], [x])
    others = exchange(sums, "chan", n_chan, 1, n_chan)
    gain, bias = call(
        functools.partial(spread_body, n_chan, n_patch),
        [shape((width, n_patch)), shape((width, n_patch))],
        [layer_norm_gain[None], layer_norm_bias[None]],
        flops=SPREAD,
    )
    args = [x, sums, *others, gain, bias, w_token_in, b_token_in[None], cot, w_token_out]
    outs = [
        shape((2, images, n_patch)),
        shape(x.shape, BF16),
        shape((images, width, hidden), BF16),
        shape((images, width, hidden), BF16),
        shape((n_patch, hidden), BF16),
    ]
    mr, normed, act, gp, send = pl.pallas_call(
        functools.partial(main_body, n_chan, channels),
        out_shape=outs,
        in_specs=[VM] * len(args),
        out_specs=[VM] * len(outs),
        scratch_shapes=[pltpu.VMEM((width, hidden), F32)] * 4 + [pltpu.VMEM((n_patch, hidden), F32)],
        name="main",
        compiler_params=LIMIT,
    )(*args)

    roles = n_dp // 2 == n_chan and side_fits(images, n_patch, hidden)
    plan = role_plan if roles else plain_plan
    return plan(x, cot, mr, normed, act, gp, send, gain, w_token_in, scale, channels)


def solution(mesh):
    placed = (P("dp", None, "chan"), P("dp", None, "chan"), P(), P(), P(), P(), P())

    return jax.shard_map(
        shards,
        mesh=mesh,
        in_specs=placed,
        out_specs=(P("dp", None, "chan"), P(), P(), P(), P("chan"), P("chan")),
        check_vma=False,
    )
```
